512 devices in a mesh: batch: 8 (over x, core), head: 2 (over z_hi), expert: 32 (over z_lo, y).
Axes of the slice: x: 4, y: 4, z: 16 (z_hi: 2, z_lo: 8; z = z_hi * 8 + z_lo), core: 2. Of those that a mesh axis runs over, the one named last changes fastest.
Arguments:
- hidden_in: bfloat16 [65536, 2048], P(('batch', 'head', 'expert')), may hold values from -6 to 6
- norm_gain: float32 [2048], replicated, may hold values from 0.25 to 1.75
- w_gate: bfloat16 [64, 2048, 384], P('expert', ('batch', 'head')), may hold values from -0.125 to 0.125
- w_up: bfloat16 [64, 2048, 384], P('expert', ('batch', 'head')), may hold values from -0.125 to 0.125
- w_down: bfloat16 [64, 384, 2048], P('expert', None, ('batch', 'head')), may hold values from -0.3125 to 0.3125
- expert_ids: int32 [65536, 2], P(('batch', 'head', 'expert')), may hold values from 0 to 63, all different within a row; in each aligned block of 128 rows (0 to 127, 128 to 255, ...) at most 6 rows name the same one
- gate_codes: int32 [65536, 2], P(('batch', 'head', 'expert')), may hold values from 4096 to 65535
- out_grad: bfloat16 [65536, 2048], P(('batch', 'head', 'expert')), may hold values from -6 to 6
Outputs:
- output: bfloat16 [65536, 2048], P(('batch', 'head', 'expert'))
- grad_in: bfloat16 [65536, 2048], P(('batch', 'head', 'expert'))
The draws below stay inside these ranges and needn't reach their ends.
Inputs may be any that keep to these rules, and one draw needn't show every extreme that they name: `expert_ids`: each row names 2 different experts; within the rows of one device no expert is named more than 6 times, a bound that some block reaches.
All inputs are finite; a program needn't handle non-finite values.
Results may differ from the reference program's by a relative error of at most 0.0055.
Values may be sent and summed in bfloat16 or wider, within the bound.
No kernel may reach another device: no remote copies, remote signals or barrier semaphores. Data moves between devices by JAX's collectives and lax.ppermute only.
A program may use at most 128 MiB of HBM per device.

```python
import math
import jax
import jax.numpy as jnp
import numpy as np
from jax import lax

D = 2048
FW = 384
TOP = 2
TOK_DEV = 128
EXPERTS = 64
CAP = 6
TOKENS = 65536


def touch_ends(values, key, low, high):
    place = [jax.random.randint(jax.random.fold_in(key, axis), (), 0, length) for axis, length in enumerate(values.shape)]
    main_axis = values.shape.index(max(values.shape))
    neighbour = place[:main_axis] + [(place[main_axis] + 1) % values.shape[main_axis]] + place[main_axis + 1:]
    return values.at[tuple(place)].set(low).at[tuple(neighbour)].set(high)


def level_of(stream_key, dims, split, least, top_value):
    gain = 1.0
    for dim, blocks in split:
        heights = jax.random.uniform(jax.random.fold_in(jax.random.fold_in(stream_key, 6), dim), (blocks,), jnp.float32, least / len(split), top_value / len(split))
        gain = gain * jnp.repeat(jnp.exp(heights), dims[dim] // blocks).reshape((-1,) + (1,) * (len(dims) - 1 - dim))
    return gain


def routed_block(stream_key, own, number, rows, count, top, most, slope):
    sequence = jax.random.permutation(stream_key, count)
    crowded, ordinary = portions_of(count, rows * top, most, slope, True), portions_of(count, rows * top, most, slope, False)
    places = jnp.arange(count)

    def named(sizes, rotation):
        used = int((sizes > 0).sum())
        fixed = max(1, used // 4)
        moved = fixed + (places - fixed + rotation * (used - fixed)) % max(1, count - fixed)
        return jnp.zeros((count,), jnp.int32).at[sequence[jnp.where(places < fixed, places, moved)]].set(jnp.asarray(sizes, jnp.int32))

    sizes = jnp.where(number % 4 == 0, named(crowded, number // 4), named(ordinary, number - number // 4 - 1))
    mixed = jax.random.permutation(jax.random.fold_in(own, 3), count)
    donor, sink = mixed[0:count // 2 * 2:2], mixed[1:count // 2 * 2:2]
    slack = jnp.minimum(sizes[donor] - 1, most - sizes[sink]) // 2
    slack = jnp.where((donor == sequence[0]) | (sink == sequence[0]) | (sizes[sink] == 0), 0, jnp.maximum(slack, 0))
    moved = jax.random.randint(jax.random.fold_in(own, 4), (count // 2,), 0, 1 << 20) % (slack + 1)
    sizes = sizes.at[donor].add(-moved).at[sink].add(moved)
    items = jnp.searchsorted(jnp.cumsum(sizes), jnp.arange(rows * top), side="right").astype(jnp.int32)
    table = items.reshape(top, rows).T
    table = table[jax.random.permutation(jax.random.fold_in(own, 1), rows)]
    rotation = jax.random.randint(jax.random.fold_in(own, 2), (rows, 1), 0, top)
    return jnp.take_along_axis(table, (jnp.arange(top)[None, :] + rotation) % top, axis=1)


def portions_of(amount, total, limit, slope, full):
    weights = [(1 << 20) // math.isqrt(rank ** slope) + 1 for rank in range(1, amount + 1)]
    largest = limit if full else min(limit, max(-(-total // amount), total * weights[0] // sum(weights)))
    least = 1 if total - largest >= amount - 1 else 0
    holding, rest = [largest] + [least] * (amount - 1), total - largest - least * (amount - 1)
    while rest > 0:
        movable = [i for i in range(1, amount) if holding[i] < largest] or [i for i in range(1, amount) if holding[i] < limit]
        pool, left = sum([weights[i] for i in movable]), rest
        for i in movable:
            more = min(limit - holding[i], max(1, left * weights[i] // pool), rest)
            holding[i] = holding[i] + more
            rest = rest - more
    return np.array(holding)


def noise(key, dims, spread, limit, shards=(), kind=jnp.bfloat16):
    array = spread * jax.random.normal(key, dims, jnp.float32)
    if shards:
        array = array * level_of(key, dims, shards, -0.22, 0.18)
    return jnp.clip(array, -limit, limit).astype(kind)


def setup_inputs(seed: int = 0) -> dict:
    splits = jax.random.split(jax.random.key(seed), 9)
    hidden_in = noise(splits[0], (TOKENS, D), 1.0, 6.0, ((0, 512),))
    norm_gain = jnp.clip(1.0 + 0.15 * jax.random.normal(splits[1], (D,), jnp.float32), 0.25, 1.75)
    w_gate = noise(splits[2], (EXPERTS, D, FW), D ** -0.5, 0.125, ((0, 32), (1, 16)))
    w_up = noise(splits[3], (EXPERTS, D, FW), D ** -0.5, 0.125, ((0, 32), (1, 16)))
    w_down = noise(splits[4], (EXPERTS, FW, D), FW ** -0.5, 0.3125, ((0, 32), (2, 16)))
    expert_ids_keys = jax.random.split(jax.random.fold_in(splits[5], 1), TOKENS // TOK_DEV)
    expert_ids_turns = jax.random.permutation(jax.random.fold_in(splits[5], 3), TOKENS // TOK_DEV)
    expert_ids = jax.vmap(lambda own, number: routed_block(jax.random.fold_in(splits[5], 2), own, number, TOK_DEV, EXPERTS, TOP, CAP, 2))(expert_ids_keys, expert_ids_turns).reshape((TOKENS, TOP))
    gate_codes = touch_ends(jax.random.randint(splits[6], (TOKENS, TOP), 4096, 65536), jax.random.fold_in(splits[6], 1), 4096, 65535).astype(jnp.int32)
    out_grad = noise(splits[7], (TOKENS, D), 1.0, 6.0, ((0, 512),))
    return dict(hidden_in=hidden_in, norm_gain=norm_gain, w_gate=w_gate, w_up=w_up, w_down=w_down, expert_ids=expert_ids, gate_codes=gate_codes, out_grad=out_grad)


epsilon = 1e-06

def slot_tables(expert_ids, expert_total, capacity):
    chosen = expert_ids.shape[1]
    routes = expert_ids.reshape(-1).astype(jnp.int32)
    route_total = routes.shape[0]
    labels = jnp.arange(expert_total, dtype=jnp.int32)
    onehot = (routes[:, None] == labels[None, :]).astype(jnp.int32)
    before = (jnp.cumsum(onehot, axis=0) - onehot).astype(jnp.int32)
    position = lax.optimization_barrier(jnp.sum(before * onehot, axis=1)).astype(jnp.int32)
    slot_ids = (routes * capacity + position).astype(jnp.int32)
    owner_rows = (jnp.arange(route_total, dtype=jnp.int32) // chosen).astype(jnp.int32)
    source_rows = jnp.zeros((expert_total * capacity,), jnp.int32).at[slot_ids].set(owner_rows)
    filled = jnp.zeros((expert_total * capacity,), jnp.int32).at[slot_ids].set(1)
    return (slot_ids, source_rows, filled)

def expert_forward(slot_rows, gate_mat, up_mat, down_mat):
    gate_pre = jnp.dot(slot_rows, gate_mat, preferred_element_type=jnp.float32)
    up_pre = jnp.dot(slot_rows, up_mat, preferred_element_type=jnp.float32)
    inner_rows = (jax.nn.silu(gate_pre) * up_pre).astype(jnp.bfloat16)
    result = jnp.dot(inner_rows, down_mat, preferred_element_type=jnp.float32).astype(jnp.bfloat16)
    return (result, gate_pre, up_pre)

def expert_backward(slot_grads, gate_pre, up_pre, gate_mat, up_mat, down_mat):
    back_grad = jnp.dot(slot_grads, down_mat.T, preferred_element_type=jnp.float32)
    sigmoid_gate = jax.nn.sigmoid(gate_pre)
    grad_gate = (back_grad * up_pre * sigmoid_gate * (1.0 + gate_pre * (1.0 - sigmoid_gate))).astype(jnp.bfloat16)
    grad_up = (back_grad * jax.nn.silu(gate_pre)).astype(jnp.bfloat16)
    grad_rows = jnp.dot(grad_gate, gate_mat.T, preferred_element_type=jnp.float32)
    grad_rows = grad_rows + jnp.dot(grad_up, up_mat.T, preferred_element_type=jnp.float32)
    return grad_rows.astype(jnp.bfloat16)

def place_weights(slot_block, weight_block):
    return jnp.zeros((EXPERTS * CAP,), jnp.float32).at[slot_block].set(weight_block)

def reference(hidden_in, norm_gain, w_gate, w_up, w_down, expert_ids, gate_codes, out_grad):
    blocks = TOKENS // TOK_DEV
    hidden_float = hidden_in.astype(jnp.float32)
    row_scale = lax.rsqrt(lax.optimization_barrier(jnp.mean(hidden_float * hidden_float, axis=1, keepdims=True)) + epsilon)
    gain_float = norm_gain.astype(jnp.float32)
    normed = (hidden_float * row_scale * gain_float).astype(jnp.bfloat16)
    code_values = gate_codes.astype(jnp.float32)
    weights = code_values / lax.optimization_barrier(jnp.sum(code_values, axis=1, keepdims=True))
    tables = jax.vmap(slot_tables, in_axes=(0, None, None))(expert_ids.reshape(blocks, TOK_DEV, TOP), EXPERTS, CAP)
    slot_ids, source_rows, filled = tables
    slot_weights = jax.vmap(place_weights)(slot_ids, weights.reshape(blocks, TOK_DEV * TOP))
    offsets = (jnp.arange(blocks, dtype=jnp.int32) * TOK_DEV)[:, None]
    token_rows = (source_rows + offsets).astype(jnp.int32)

    def one_expert(totals, members):
        gate_mat, up_mat, down_mat, expert_index = members
        start = (expert_index * CAP).astype(jnp.int32)
        rows_index = lax.dynamic_slice_in_dim(token_rows, start, CAP, 1).reshape(-1)
        live = lax.dynamic_slice_in_dim(filled, start, CAP, 1).reshape(-1)
        share = lax.dynamic_slice_in_dim(slot_weights, start, CAP, 1).reshape(-1)
        keep = (live == 1)[:, None]
        nothing = jnp.zeros((), jnp.bfloat16)
        slot_rows = jnp.where(keep, normed[rows_index], nothing)
        slot_grads = jnp.where(keep, out_grad[rows_index], nothing)
        result, gate_pre, up_pre = expert_forward(slot_rows, gate_mat, up_mat, down_mat)
        grad_rows = expert_backward(slot_grads, gate_pre, up_pre, gate_mat, up_mat, down_mat)
        mixture, grad_normed = totals
        mixture = mixture.at[rows_index].add(share[:, None] * result.astype(jnp.float32))
        grad_normed = grad_normed.at[rows_index].add(share[:, None] * grad_rows.astype(jnp.float32))
        return ((mixture, grad_normed), None)
    start_totals = (jnp.zeros((TOKENS, D), jnp.float32), jnp.zeros((TOKENS, D), jnp.float32))
    members = (w_gate, w_up, w_down, jnp.arange(EXPERTS, dtype=jnp.int32))
    final_totals = lax.scan(one_expert, start_totals, members)[0]
    mixture, grad_normed = final_totals
    output = (hidden_float + mixture).astype(jnp.bfloat16)
    scaled = gain_float * grad_normed
    inner_mean = lax.optimization_barrier(jnp.mean(scaled * hidden_float, axis=1, keepdims=True))
    grad_in = out_grad.astype(jnp.float32) + row_scale * scaled - hidden_float * (row_scale * row_scale * row_scale) * inner_mean
    return (output, grad_in.astype(jnp.bfloat16))
```

```python
import numpy as np
import jax
import jax.numpy as jnp
from jax import lax
from jax.experimental import pallas as pl
from jax.experimental.pallas import tpu as pltpu
from jax.sharding import Mesh, PartitionSpec as P

epsilon = 1e-06
BF = jnp.bfloat16
F32 = jnp.float32
I32 = jnp.int32
VMEM = pltpu.VMEM
LIMIT = 56 * 1024 * 1024

X, C, H, B, A, Y = 4, 2, 2, 2, 4, 4
PEERS = X * C * Y
TOK, D, FW, CAP = 128, 2048, 384, 6
PER = 4 * CAP
ROWS = PEERS * PER
GROUPS = 4
GROUP = ROWS // GROUPS
KIND = GROUP // 4
SLOTS = GROUPS * KIND


def sort_matrix():
    natural = np.arange(GROUP)
    place = (natural % PER) // CAP * KIND + natural // PER * CAP + natural % CAP
    to_natural = np.zeros((GROUP, GROUP), np.float32)
    to_natural[natural, place] = 1.0
    return to_natural


def whole(n):
    return [pl.BlockSpec(memory_space=VMEM)] * n


def params(**more):
    return pltpu.CompilerParams(vmem_limit_bytes=LIMIT, **more)


def split_kernel(gate_ref, up_ref, down_ref, out_ref):
    for e in range(2):
        for q in range(A):
            for m, ref in enumerate((gate_ref, up_ref)):
                for f in range(3):
                    out_ref[q, e, m, f * 32 : (f + 1) * 32, :] = ref[
                        e, q * 32 : (q + 1) * 32, f * 128 : (f + 1) * 128
                    ]
            out_ref[q, e, 2] = down_ref[e, q * 96 : (q + 1) * 96, :]


def split_weights(w_gate, w_up, w_down):
    return pl.pallas_call(
        split_kernel,
        out_shape=jax.ShapeDtypeStruct((A, 2, 3, 96, 128), BF),
        in_specs=whole(3),
        out_specs=pl.BlockSpec(memory_space=VMEM),
        compiler_params=params(),
        name="split_weights",
    )(w_gate, w_up, w_down)


def route_rows(ids0, ids1):
    labels = lax.broadcasted_iota(I32, (64, TOK), 0)
    m0, m1 = labels == ids0, labels == ids1
    one, zero = jnp.ones((64, TOK), F32), jnp.zeros((64, TOK), F32)
    both = (jnp.where(m0, one, zero) + jnp.where(m1, one, zero)).astype(BF)
    earlier = jnp.where(
        lax.broadcasted_iota(I32, (TOK, TOK), 0) < lax.broadcasted_iota(I32, (TOK, TOK), 1),
        jnp.ones((TOK, TOK), F32),
        jnp.zeros((TOK, TOK), F32),
    ).astype(BF)
    before = jnp.dot(both, earlier, preferred_element_type=F32)

    def row(ids, mask):
        position = jnp.sum(jnp.where(mask, before, zero), axis=0, keepdims=True).astype(I32)
        x, b = (ids >> 3) & 3, ids >> 5
        y, c = (ids >> 1) & 3, ids & 1
        return ((x * C + c) * Y + y) * PER + b * CAP + position

    return row(ids0, m0), row(ids1, m1)


def row_scale_of(hidden):
    return lax.rsqrt(jnp.mean(hidden * hidden, axis=1, keepdims=True) + epsilon)


def dispatch_kernel(ids_ref, hidden_ref, gain_ref, grad_ref, out_ref):
    hidden = hidden_ref[...].astype(F32)
    normed = (hidden * row_scale_of(hidden) * gain_ref[...]).astype(BF)
    both = jnp.concatenate([normed, grad_ref[...]], axis=0)
    r0, r1 = route_rows(ids_ref[0:1, :], ids_ref[1:2, :])
    one, zero = jnp.ones((GROUP, TOK), F32), jnp.zeros((GROUP, TOK), F32)
    for g in range(GROUPS):
        at = lax.broadcasted_iota(I32, (GROUP, TOK), 0) + g * GROUP
        picks = []
        for shift in (0, 2 * CAP):
            hit = (at == r0 + shift) | (at == r1 + shift)
            picks.append(jnp.where(hit, one, zero).astype(BF))
        chosen = jnp.concatenate(picks, axis=1)
        out_ref[g * GROUP : (g + 1) * GROUP, :] = jnp.dot(
            chosen, both, preferred_element_type=F32
        ).astype(BF)


def dispatch(ids, hidden, gain, grad):
    return pl.pallas_call(
        dispatch_kernel,
        out_shape=jax.ShapeDtypeStruct((ROWS, D), BF),
        in_specs=whole(4),
        out_specs=pl.BlockSpec(memory_space=VMEM),
        compiler_params=params(),
        name="dispatch",
    )(ids, hidden, gain, grad)


def sort_kernel(to_sorted_ref, rows_ref, out_ref):
    for g in range(GROUPS):
        block = jnp.dot(
            to_sorted_ref[...],
            rows_ref[g * GROUP : (g + 1) * GROUP, :],
            preferred_element_type=F32,
        ).astype(BF)
        for k in range(4):
            out_ref[k, g * KIND : (g + 1) * KIND, :] = block[k * KIND : (k + 1) * KIND, :]


def sort_rows(to_sorted, rows):
    return pl.pallas_call(
        sort_kernel,
        out_shape=jax.ShapeDtypeStruct((4, SLOTS, D), BF),
        in_specs=whole(2),
        out_specs=pl.BlockSpec(memory_space=VMEM),
        compiler_params=params(),
        name="sort_rows",
    )(to_sorted, rows)


def expert_kernel(rows_ref, to_natural_ref, w_ref, out_ref, in_mats, down_mat, sems):
    copies = []
    for b in range(B):
        mine = []
        for h in range(H):
            for q in range(A):
                z = (h * B + b) * A + q
                for m in range(2):
                    for f in range(3):
                        mine.append(
                            pltpu.make_async_copy(
                                w_ref.at[z, :, m, pl.ds(f * 32, 32), :],
                                in_mats.at[b, m, :, h, q, :, pl.ds(f * 128, 128)],
                                sems.at[b],
                            )
                        )
                mine.append(
                    pltpu.make_async_copy(
                        w_ref.at[z, :, 2, :, :],
                        down_mat.at[b, :, h, pl.ds(q * 96, 96), :],
                        sems.at[b],
                    )
                )
        copies.append(mine)
    for mine in copies:
        for c in mine:
            c.start()
    inner, d_gate, d_up = [], [], []
    for b in range(B):
        for c in copies[b]:
            c.wait()
        rows = rows_ref[b]
        gate_pre = jnp.dot(rows, in_mats[b, 0].reshape(D, FW), preferred_element_type=F32)
        up_pre = jnp.dot(rows, in_mats[b, 1].reshape(D, FW), preferred_element_type=F32)
        back = jnp.zeros((SLOTS, FW), F32)
        for k in range(8):
            chunk = jnp.concatenate([down_mat[b, k, 0], down_mat[b, k, 1]], axis=1)
            back = back + lax.dot_general(
                rows_ref[2 + b, :, k * 256 : (k + 1) * 256],
                chunk,
                (((1,), (1,)), ((), ())),
                preferred_element_type=F32,
            )
        s = jax.nn.sigmoid(gate_pre)
        silu = gate_pre * s
        inner.append((silu * up_pre).astype(BF))
        d_gate.append((back * up_pre * s * (1.0 + gate_pre * (1.0 - s))).astype(BF))
        d_up.append((back * silu).astype(BF))
    for k in range(8):
        parts = []
        for b in range(B):
            chunk = jnp.concatenate([down_mat[b, k, 0], down_mat[b, k, 1]], axis=1)
            parts.append(jnp.dot(inner[b], chunk, preferred_element_type=F32).astype(BF))
        for b in range(B):
            total = lax.dot_general(
                d_gate[b],
                in_mats[b, 0, k].reshape(256, FW),
                (((1,), (1,)), ((), ())),
                preferred_element_type=F32,
            ) + lax.dot_general(
                d_up[b],
                in_mats[b, 1, k].reshape(256, FW),
                (((1,), (1,)), ((), ())),
                preferred_element_type=F32,
            )
            parts.append(total.astype(BF))
        for g in range(GROUPS):
            block = jnp.concatenate([p[g * KIND : (g + 1) * KIND] for p in parts], axis=0)
            out_ref[g * GROUP : (g + 1) * GROUP, k * 256 : (k + 1) * 256] = jnp.dot(
                to_natural_ref[...], block, preferred_element_type=F32
            ).astype(BF)


def experts(rows, to_natural, weights):
    return pl.pallas_call(
        expert_kernel,
        out_shape=jax.ShapeDtypeStruct((ROWS, D), BF),
        in_specs=whole(2) + [pl.BlockSpec(memory_space=pl.ANY)],
        out_specs=pl.BlockSpec(memory_space=VMEM),
        scratch_shapes=[
            VMEM((B, 2, 8, H, A, 32, FW), BF),
            VMEM((B, 8, H, FW, 128), BF),
            pltpu.SemaphoreType.DMA((B,)),
        ],
        compiler_params=params(),
        name="experts",
    )(rows, to_natural, weights)


def combine_kernel(ids_ref, codes_ref, ret_ref, hidden_ref, gain_ref, grad_ref, out_ref, gin_ref):
    r0, r1 = route_rows(ids_ref[0:1, :], ids_ref[1:2, :])
    codes = codes_ref[...].astype(F32)
    weights = codes / (codes[0:1, :] + codes[1:2, :])
    lines = jnp.concatenate(
        [r0.astype(F32), r1.astype(F32), weights, jnp.zeros((TOK - 4, TOK), F32)], axis=0
    )
    columns = jnp.transpose(lines)
    c0, c1 = columns[:, 0:1].astype(I32), columns[:, 1:2].astype(I32)
    w0, w1 = columns[:, 2:3], columns[:, 3:4]
    at = lax.broadcasted_iota(I32, (TOK, ROWS), 1)
    one, zero = jnp.ones((TOK, ROWS), F32), jnp.zeros((TOK, ROWS), F32)
    chosen = jnp.concatenate(
        [
            jnp.where(at == c + shift, one, zero).astype(BF)
            for shift in (0, 2 * CAP)
            for c in (c0, c1)
        ],
        axis=0,
    )
    picked = jnp.dot(chosen, ret_ref[...], preferred_element_type=F32)
    mixture = picked[0:TOK] * w0 + picked[TOK : 2 * TOK] * w1
    grad_normed = picked[2 * TOK : 3 * TOK] * w0 + picked[3 * TOK :] * w1
    hidden = hidden_ref[...].astype(F32)
    row_scale = row_scale_of(hidden)
    out_ref[...] = (hidden + mixture).astype(BF)
    scaled = gain_ref[...] * grad_normed
    inner_mean = jnp.mean(scaled * hidden, axis=1, keepdims=True)
    gin_ref[...] = (
        grad_ref[...].astype(F32)
        + row_scale * scaled
        - hidden * ((row_scale * row_scale * row_scale) * inner_mean)
    ).astype(BF)


def combine(ids, codes, returned, hidden, gain, grad):
    shape = jax.ShapeDtypeStruct((TOK, D), BF)
    return pl.pallas_call(
        combine_kernel,
        out_shape=(shape, shape),
        in_specs=whole(6),
        out_specs=tuple(whole(2)),
        compiler_params=params(),
        name="combine",
    )(ids, codes, returned, hidden, gain, grad)


def exchange(rows):
    blocks = rows.reshape(PEERS, PER, D)
    return lax.all_to_all(blocks, ("X", "C", "Y"), 0, 0, tiled=True).reshape(ROWS, D)


def body(hidden_in, norm_gain, w_gate, w_up, w_down, expert_ids, gate_codes, out_grad):
    gain = norm_gain.reshape(1, D)
    ids, codes = expert_ids.T, gate_codes.T
    to_natural = sort_matrix()
    pieces = split_weights(w_gate, w_up, w_down)
    pieces = lax.all_to_all(pieces, "A", 0, 0, tiled=True)
    pieces = pieces.reshape(X * C, 3, 96, 128)
    pieces = lax.all_to_all(pieces, ("X", "C"), 0, 0, tiled=True)
    weights = lax.all_gather(pieces, ("H", "B", "A"), axis=0, tiled=False)
    arrived = exchange(dispatch(ids, hidden_in, gain, out_grad))
    rows = sort_rows(jnp.asarray(to_natural.T, BF), arrived)
    results = experts(rows, jnp.asarray(to_natural, BF), weights)
    returned = exchange(results)
    return combine(ids, codes, returned, hidden_in, gain, out_grad)


def solution(mesh):
    fine = Mesh(mesh.devices.reshape(X, C, H, B, A, Y), ("X", "C", "H", "B", "A", "Y"))
    tokens = P(("X", "C", "H", "B", "A", "Y"), None)
    owner, feature = ("B", "A", "Y"), ("X", "C", "H")
    in_specs = (
        tokens,
        P(),
        P(owner, feature, None),
        P(owner, feature, None),
        P(owner, None, feature),
        tokens,
        tokens,
        tokens,
    )
    return jax.shard_map(
        body, mesh=fine, in_specs=in_specs, out_specs=(tokens, tokens), check_vma=False
    )
```

```python
import functools

import numpy as np
import jax
import jax.numpy as jnp
from jax import lax
from jax.experimental import pallas as pl
from jax.experimental.pallas import tpu as pltpu
from jax.sharding import Mesh, PartitionSpec as P

epsilon = 1e-06
BF = jnp.bfloat16
F32 = jnp.float32
I32 = jnp.int32
VMEM = pltpu.VMEM
LIMIT = 56 * 1024 * 1024

X, C, H, B, A, Y = 4, 2, 2, 2, 4, 4
PEERS = X * C * Y
TOK, D, FW, CAP = 128, 2048, 384, 6
PER = 4 * CAP
ROWS = PEERS * PER
GROUPS = 4
GROUP = ROWS // GROUPS
KIND = GROUP // 4
SLOTS = GROUPS * KIND


def sort_matrix():
    natural = np.arange(GROUP)
    place = (natural % PER) // CAP * KIND + natural // PER * CAP + natural % CAP
    to_natural = np.zeros((GROUP, GROUP), np.float32)
    to_natural[natural, place] = 1.0
    return to_natural


def whole(n):
    return [pl.BlockSpec(memory_space=VMEM)] * n


def params(**more):
    return pltpu.CompilerParams(vmem_limit_bytes=LIMIT, **more)


def split_kernel(*refs):
    gate_ref, up_ref, down_ref = refs[:3]
    x, c = lax.axis_index("X"), lax.axis_index("C")
    for r in range(X):
        for s in range(C):
            out_ref = refs[3 + r * C + s]
            part = ((c + s) & 1) * A + ((x + r) & 3)
            for m, ref in enumerate((gate_ref, up_ref)):
                for f in range(3):
                    out_ref[m, f * 16 : (f + 1) * 16, :] = ref[
                        0, pl.ds(pl.multiple_of(part * 16, 16), 16), f * 128 : (f + 1) * 128
                    ]
            out_ref[2] = down_ref[0, pl.ds(pl.multiple_of(part * 48, 16), 48), :]


def split_weights(e, w_gate, w_up, w_down):
    shape = jax.ShapeDtypeStruct((3, 48, 128), BF)
    return pl.pallas_call(
        split_kernel,
        grid=(1,),
        out_shape=(shape,) * 8,
        in_specs=[
            pl.BlockSpec((1, 128, FW), lambda i: (e, 0, 0)),
            pl.BlockSpec((1, 128, FW), lambda i: (e, 0, 0)),
            pl.BlockSpec((1, FW, 128), lambda i: (e, 0, 0)),
        ],
        out_specs=(pl.BlockSpec((3, 48, 128), lambda i: (0, 0, 0)),) * 8,
        compiler_params=params(),
        name=f"split_weights_{e}",
    )(w_gate, w_up, w_down)


def place_kernel(*refs):
    out_ref, sem = refs[8:]
    b, a = lax.axis_index("B"), lax.axis_index("A")
    copies = []
    for r in range(X):
        for s in range(C):
            to = out_ref.at[((a - r) & 3) * C + ((b - s) & 1)]
            copies.append(pltpu.make_async_copy(refs[r * C + s], to, sem))
    for copy in copies:
        copy.start()
    for copy in copies:
        copy.wait()


def place(e, pieces):
    return pl.pallas_call(
        place_kernel,
        out_shape=jax.ShapeDtypeStruct((X * C, 3, 48, 128), BF),
        in_specs=[pl.BlockSpec(memory_space=pl.ANY)] * 8,
        out_specs=pl.BlockSpec(memory_space=VMEM),
        scratch_shapes=[pltpu.SemaphoreType.DMA],
        compiler_params=params(),
        name=f"place_{e}",
    )(*pieces)


def send_home(pieces):
    moved = []
    for r in range(X):
        for s in range(C):
            pairs = []
            for x in range(X):
                for c in range(C):
                    for b in range(B):
                        for a in range(A):
                            home = ((a * C + b) * B + (c + s) % C) * A + (x + r) % X
                            pairs.append((((x * C + c) * B + b) * A + a, home))
            moved.append(lax.ppermute(pieces[r * C + s], ("X", "C", "B", "A"), pairs))
    return moved


def places(ids0, ids1):
    labels = lax.broadcasted_iota(I32, (64, TOK), 0)
    m0, m1 = labels == ids0, labels == ids1
    one, zero = jnp.ones((64, TOK), F32), jnp.zeros((64, TOK), F32)
    both = (jnp.where(m0, one, zero) + jnp.where(m1, one, zero)).astype(BF)
    earlier = jnp.where(
        lax.broadcasted_iota(I32, (TOK, TOK), 0) < lax.broadcasted_iota(I32, (TOK, TOK), 1),
        jnp.ones((TOK, TOK), F32),
        jnp.zeros((TOK, TOK), F32),
    ).astype(BF)
    before = jnp.dot(both, earlier, preferred_element_type=F32)

    def row(ids, mask):
        position = jnp.sum(jnp.where(mask, before, zero), axis=0, keepdims=True).astype(I32)
        a, b, y = (ids >> 3) & 3, ids >> 5, (ids >> 1) & 3
        return (a * C + b) * Y + y, position, ids & 1

    return row(ids0, m0), row(ids1, m1)


def route_rows(ids0, ids1):
    return tuple(peer * PER + e * CAP + position for peer, position, e in places(ids0, ids1))


def row_scale_of(hidden):
    return lax.rsqrt(jnp.mean(hidden * hidden, axis=1, keepdims=True) + epsilon)


def dispatch_kernel(ids_ref, hidden_ref, gain_ref, grad_ref, out_ref):
    hidden = hidden_ref[...].astype(F32)
    normed = (hidden * row_scale_of(hidden) * gain_ref[...]).astype(BF)
    both = jnp.concatenate([normed, grad_ref[...]], axis=0)
    r0, r1 = route_rows(ids_ref[0:1, :], ids_ref[1:2, :])
    one, zero = jnp.ones((GROUP, TOK), F32), jnp.zeros((GROUP, TOK), F32)
    for g in range(GROUPS):
        at = lax.broadcasted_iota(I32, (GROUP, TOK), 0) + g * GROUP
        picks = []
        for shift in (0, 2 * CAP):
            hit = (at == r0 + shift) | (at == r1 + shift)
            picks.append(jnp.where(hit, one, zero).astype(BF))
        chosen = jnp.concatenate(picks, axis=1)
        out_ref[g * GROUP : (g + 1) * GROUP, :] = jnp.dot(
            chosen, both, preferred_element_type=F32
        ).astype(BF)


def dispatch(ids, hidden, gain, grad):
    return pl.pallas_call(
        dispatch_kernel,
        out_shape=jax.ShapeDtypeStruct((ROWS, D), BF),
        in_specs=whole(4),
        out_specs=pl.BlockSpec(memory_space=VMEM),
        compiler_params=params(),
        name="dispatch",
    )(ids, hidden, gain, grad)


def sort_kernel(to_sorted_ref, rows_ref, out_ref):
    for g in range(GROUPS):
        block = jnp.dot(
            to_sorted_ref[...],
            rows_ref[g * GROUP : (g + 1) * GROUP, :],
            preferred_element_type=F32,
        ).astype(BF)
        for k in range(4):
            out_ref[k, g * KIND : (g + 1) * KIND, :] = block[k * KIND : (k + 1) * KIND, :]


def sort_rows(to_sorted, rows):
    return pl.pallas_call(
        sort_kernel,
        out_shape=jax.ShapeDtypeStruct((4, SLOTS, D), BF),
        in_specs=whole(2),
        out_specs=pl.BlockSpec(memory_space=VMEM),
        compiler_params=params(),
        name="sort_rows",
    )(to_sorted, rows)


def expert_kernel(e, all_rows_ref, to_natural_ref, w_ref, out_hbm, rows_ref, in_mats, down_mat, out_ref, row_sem, w_sems, out_sem):
    row_copies = [
        pltpu.make_async_copy(all_rows_ref.at[2 * kind + e], rows_ref.at[kind], row_sem)
        for kind in range(2)
    ]
    in_copies, down_copies = [], []
    for h in range(H):
        for part in range(8):
            z = h * 8 + part
            for m in range(2):
                for f in range(3):
                    in_copies.append(
                        pltpu.make_async_copy(
                            w_ref.at[z, :, m, pl.ds(f * 16, 16), :],
                            in_mats.at[m, :, h, part, :, pl.ds(f * 128, 128)],
                            w_sems.at[0],
                        )
                    )
            down_copies.append(
                pltpu.make_async_copy(
                    w_ref.at[z, :, 2, :, :],
                    down_mat.at[:, h, pl.ds(part * 48, 48), :],
                    w_sems.at[1],
                )
            )
    for c in row_copies + down_copies + in_copies:
        c.start()
    for c in row_copies + down_copies:
        c.wait()

    def down_chunk(k):
        return jnp.concatenate([down_mat[k, 0], down_mat[k, 1]], axis=1)

    across = (((1,), (1,)), ((), ()))
    back = jnp.zeros((SLOTS, FW), F32)
    for k in range(8):
        back = back + lax.dot_general(
            rows_ref[1, :, k * 256 : (k + 1) * 256],
            down_chunk(k),
            across,
            preferred_element_type=F32,
        )
    for c in in_copies:
        c.wait()
    rows = rows_ref[0]
    gate_pre = jnp.dot(rows, in_mats[0].reshape(D, FW), preferred_element_type=F32)
    up_pre = jnp.dot(rows, in_mats[1].reshape(D, FW), preferred_element_type=F32)
    s = jax.nn.sigmoid(gate_pre)
    silu = gate_pre * s
    inner = (silu * up_pre).astype(BF)
    d_gate = (back * up_pre * s * (1.0 + gate_pre * (1.0 - s))).astype(BF)
    d_up = (back * silu).astype(BF)
    out_copies = []
    for j in range(4):
        parts = []
        for k in (j, j + 4):
            result = jnp.dot(inner, down_chunk(k), preferred_element_type=F32)
            grads = lax.dot_general(
                d_gate, in_mats[0, k].reshape(256, FW), across, preferred_element_type=F32
            ) + lax.dot_general(
                d_up, in_mats[1, k].reshape(256, FW), across, preferred_element_type=F32
            )
            parts += [result.astype(BF), grads.astype(BF)]
        for g in range(GROUPS):
            block = jnp.concatenate([p[g * KIND : (g + 1) * KIND] for p in parts], axis=0)
            out_ref[j, g * GROUP : (g + 1) * GROUP, :] = jnp.dot(
                to_natural_ref[...], block, preferred_element_type=F32
            ).astype(BF)
        copy = pltpu.make_async_copy(
            out_ref.at[j], out_hbm.at[:, pl.ds(j * 256, 256)], out_sem.at[j]
        )
        copy.start()
        out_copies.append(copy)
    for copy in out_copies:
        copy.wait()


def experts(e, rows, to_natural, weights):
    anywhere = pl.BlockSpec(memory_space=pl.ANY)
    return pl.pallas_call(
        functools.partial(expert_kernel, e),
        out_shape=jax.ShapeDtypeStruct((ROWS, D // 2), BF),
        in_specs=[anywhere, pl.BlockSpec(memory_space=VMEM), anywhere],
        out_specs=anywhere,
        scratch_shapes=[
            VMEM((2, SLOTS, D), BF),
            VMEM((2, 8, H, 8, 16, FW), BF),
            VMEM((8, H, FW, 128), BF),
            VMEM((4, ROWS, 256), BF),
            pltpu.SemaphoreType.DMA,
            pltpu.SemaphoreType.DMA((2,)),
            pltpu.SemaphoreType.DMA((4,)),
        ],
        compiler_params=params(),
        name=f"experts_{e}",
    )(rows, to_natural, weights)


def gathered(e, ids_ref, codes_ref, to_sorted_ref, ret_hbm, ret_ref, sem):
    copy = pltpu.make_async_copy(ret_hbm, ret_ref, sem)
    copy.start()
    (p0, s0, e0), (p1, s1, e1) = places(ids_ref[0:1, :], ids_ref[1:2, :])
    codes = codes_ref[...].astype(F32)
    weights = codes / (codes[0:1, :] + codes[1:2, :])
    slot0 = jnp.where(e0 == e, p0 * CAP + s0, -1)
    slot1 = jnp.where(e1 == e, p1 * CAP + s1, -1)
    lines = jnp.concatenate(
        [slot0.astype(F32), slot1.astype(F32), weights, jnp.zeros((TOK - 4, TOK), F32)], axis=0
    )
    columns = jnp.transpose(lines)
    w0, w1 = columns[:, 2:3], columns[:, 3:4]
    at = lax.broadcasted_iota(I32, (TOK, SLOTS), 1)
    one, zero = jnp.ones((TOK, SLOTS), F32), jnp.zeros((TOK, SLOTS), F32)
    chosen = jnp.concatenate(
        [
            jnp.where(at == columns[:, k : k + 1].astype(I32), one, zero).astype(BF)
            for k in range(2)
        ],
        axis=0,
    )
    copy.wait()
    blocks = [
        jnp.dot(
            to_sorted_ref[...],
            ret_ref[g * GROUP : (g + 1) * GROUP, :],
            preferred_element_type=F32,
        ).astype(BF)
        for g in range(GROUPS)
    ]
    found = []
    for kind in range(2):
        halves = []
        for half in range(2):
            at_row = (half * 2 + kind) * KIND
            values = jnp.concatenate([v[at_row : at_row + KIND] for v in blocks], axis=0)
            picked = jnp.dot(chosen, values, preferred_element_type=F32)
            halves.append(picked[:TOK] * w0 + picked[TOK:] * w1)
        found.append(halves)
    return found


def first_kernel(ret_hbm, ids_ref, codes_ref, to_sorted_ref, mix_ref, grad_ref, *scratch):
    found = gathered(0, ids_ref, codes_ref, to_sorted_ref, ret_hbm, *scratch)
    for half in range(2):
        mix_ref[:, half * 1024 : (half + 1) * 1024] = found[0][half]
        grad_ref[:, half * 1024 : (half + 1) * 1024] = found[1][half]


RETURNED = [VMEM((ROWS, D // 2), BF), pltpu.SemaphoreType.DMA]


def first_sums(*operands):
    shape = jax.ShapeDtypeStruct((TOK, D), F32)
    return pl.pallas_call(
        first_kernel,
        out_shape=(shape, shape),
        in_specs=[pl.BlockSpec(memory_space=pl.ANY)] + whole(3),
        out_specs=tuple(whole(2)),
        scratch_shapes=RETURNED,
        compiler_params=params(),
        name="first_sums",
    )(*operands)


def last_kernel(
    ret_hbm, ids_ref, codes_ref, to_sorted_ref, mix_ref, gn_ref, hidden_ref, gain_ref, grad_ref,
    out_ref, gin_ref, *scratch,
):
    found = gathered(1, ids_ref, codes_ref, to_sorted_ref, ret_hbm, *scratch)
    mixture = mix_ref[...] + jnp.concatenate(found[0], axis=1)
    grad_normed = gn_ref[...] + jnp.concatenate(found[1], axis=1)
    hidden = hidden_ref[...].astype(F32)
    row_scale = row_scale_of(hidden)
    out_ref[...] = (hidden + mixture).astype(BF)
    scaled = gain_ref[...] * grad_normed
    inner_mean = jnp.mean(scaled * hidden, axis=1, keepdims=True)
    gin_ref[...] = (
        grad_ref[...].astype(F32)
        + row_scale * scaled
        - hidden * ((row_scale * row_scale * row_scale) * inner_mean)
    ).astype(BF)


def last_sums(*operands):
    shape = jax.ShapeDtypeStruct((TOK, D), BF)
    return pl.pallas_call(
        last_kernel,
        out_shape=(shape, shape),
        in_specs=[pl.BlockSpec(memory_space=pl.ANY)] + whole(8),
        out_specs=tuple(whole(2)),
        scratch_shapes=RETURNED,
        compiler_params=params(),
        name="last_sums",
    )(*operands)


def exchange(rows):
    blocks = rows.reshape(PEERS, PER, rows.shape[1])
    return lax.all_to_all(blocks, ("X", "C", "Y"), 0, 0, tiled=True).reshape(rows.shape)


def body(hidden_in, norm_gain, w_gate, w_up, w_down, expert_ids, gate_codes, out_grad):
    gain = norm_gain.reshape(1, D)
    ids, codes = expert_ids.T, gate_codes.T
    matrix = sort_matrix()
    to_natural, to_sorted = jnp.asarray(matrix, BF), jnp.asarray(matrix.T, BF)
    weights = []
    for e in range(2):
        pieces = place(e, send_home(split_weights(e, w_gate, w_up, w_down)))
        weights.append(lax.all_gather(pieces, ("H", "B", "A"), axis=0, tiled=False))
    arrived = exchange(dispatch(ids, hidden_in, gain, out_grad))
    rows = sort_rows(to_sorted, arrived)
    returned = exchange(experts(0, rows, to_natural, weights[0]))
    mixture, grad_normed = first_sums(returned, ids, codes, to_sorted)
    returned = exchange(experts(1, rows, to_natural, weights[1]))
    return last_sums(
        returned, ids, codes, to_sorted, mixture, grad_normed, hidden_in, gain, out_grad
    )


def solution(mesh):
    fine = Mesh(mesh.devices.reshape(X, C, H, B, A, Y), ("X", "C", "H", "B", "A", "Y"))
    tokens = P(("X", "C", "H", "B", "A", "Y"), None)
    owner, feature = ("B", "A", "Y"), ("X", "C", "H")
    in_specs = (
        tokens,
        P(),
        P(owner, feature, None),
        P(owner, feature, None),
        P(owner, None, feature),
        tokens,
        tokens,
        tokens,
    )
    return jax.shard_map(
        body, mesh=fine, in_specs=in_specs, out_specs=(tokens, tokens), check_vma=False
    )
```

```python
import numpy as np
import jax
import jax.numpy as jnp
from jax import lax
from jax.experimental import pallas as pl
from jax.experimental.pallas import tpu as pltpu
from jax.sharding import Mesh, PartitionSpec as P

epsilon = 1e-06
BF = jnp.bfloat16
F32 = jnp.float32
I32 = jnp.int32
VMEM = pltpu.VMEM
MIB = 1024 * 1024

X, C, H, B, A, Y = 4, 2, 2, 2, 4, 4
PEERS = X * C * Y
TOK, D, FW, CAP = 128, 2048, 384, 6
PER = 4 * CAP
ROWS = PEERS * PER
GROUPS = 4
GROUP = ROWS // GROUPS
KIND = GROUP // 4
SLOTS = GROUPS * KIND


def sort_matrix():
    natural = np.arange(GROUP)
    place = (natural % PER) // CAP * KIND + natural // PER * CAP + natural % CAP
    to_natural = np.zeros((GROUP, GROUP), np.float32)
    to_natural[natural, place] = 1.0
    return to_natural


def whole(n):
    return [pl.BlockSpec(memory_space=VMEM)] * n


def params(mib=24):
    return pltpu.CompilerParams(vmem_limit_bytes=mib * MIB)


def split_kernel(gate_ref, up_ref, down_ref, *out_refs):
    x = lax.axis_index("X")
    for r in range(X):
        q = (x + r) & 3
        for e in range(2):
            for m, ref in enumerate((gate_ref, up_ref)):
                for f in range(3):
                    out_refs[r][e, m, f * 32 : (f + 1) * 32, :] = ref[
                        e, pl.ds(pl.multiple_of(q * 32, 32), 32), f * 128 : (f + 1) * 128
                    ]
            out_refs[r][e, 2] = down_ref[e, pl.ds(pl.multiple_of(q * 96, 32), 96), :]


def split_weights(w_gate, w_up, w_down):
    return pl.pallas_call(
        split_kernel,
        out_shape=(jax.ShapeDtypeStruct((2, 3, 96, 128), BF),) * X,
        in_specs=whole(3),
        out_specs=tuple(whole(X)),
        compiler_params=params(),
        name="split_weights",
    )(w_gate, w_up, w_down)


def send_home(pieces):
    moved = []
    for r in range(X):
        pairs = [(x * A + a, a * A + (x + r) % X) for x in range(X) for a in range(A)]
        moved.append(lax.ppermute(pieces[r], ("X", "A"), pairs))
    return moved


def place_kernel(*refs):
    out_ref, sem = refs[X:]
    a = lax.axis_index("A")
    copies = [
        pltpu.make_async_copy(refs[r], out_ref.at[:, (a - r) & 3], sem) for r in range(X)
    ]
    for copy in copies:
        copy.start()
    for copy in copies:
        copy.wait()


def place(pieces):
    return pl.pallas_call(
        place_kernel,
        out_shape=pltpu.VMEM((2, X, 3, 96, 128), BF),
        in_specs=[pl.BlockSpec(memory_space=pl.ANY)] * X,
        out_specs=pl.BlockSpec(memory_space=VMEM),
        scratch_shapes=[pltpu.SemaphoreType.DMA],
        compiler_params=params(),
        name="place",
    )(*pieces)


def route_rows(ids0, ids1):
    labels = lax.broadcasted_iota(I32, (64, TOK), 0)
    m0, m1 = labels == ids0, labels == ids1
    one, zero = jnp.ones((64, TOK), F32), jnp.zeros((64, TOK), F32)
    both = (jnp.where(m0, one, zero) + jnp.where(m1, one, zero)).astype(BF)
    earlier = jnp.where(
        lax.broadcasted_iota(I32, (TOK, TOK), 0) < lax.broadcasted_iota(I32, (TOK, TOK), 1),
        jnp.ones((TOK, TOK), F32),
        jnp.zeros((TOK, TOK), F32),
    ).astype(BF)
    before = jnp.dot(both, earlier, preferred_element_type=F32)

    def row(ids, mask):
        position = jnp.sum(jnp.where(mask, before, zero), axis=0, keepdims=True).astype(I32)
        x, b = (ids >> 3) & 3, ids >> 5
        y, c = (ids >> 1) & 3, ids & 1
        return ((x * C + c) * Y + y) * PER + b * CAP + position

    return row(ids0, m0), row(ids1, m1)


def row_scale_of(hidden):
    return lax.rsqrt(jnp.mean(hidden * hidden, axis=1, keepdims=True) + epsilon)


def dispatch_kernel(ids_ref, hidden_ref, gain_ref, grad_ref, out_ref):
    hidden = hidden_ref[...].astype(F32)
    normed = (hidden * row_scale_of(hidden) * gain_ref[...]).astype(BF)
    both = jnp.concatenate([normed, grad_ref[...]], axis=0)
    r0, r1 = route_rows(ids_ref[0:1, :], ids_ref[1:2, :])
    one, zero = jnp.ones((GROUP, TOK), F32), jnp.zeros((GROUP, TOK), F32)
    for g in range(GROUPS):
        at = lax.broadcasted_iota(I32, (GROUP, TOK), 0) + g * GROUP
        picks = []
        for shift in (0, 2 * CAP):
            hit = (at == r0 + shift) | (at == r1 + shift)
            picks.append(jnp.where(hit, one, zero).astype(BF))
        chosen = jnp.concatenate(picks, axis=1)
        out_ref[g * GROUP : (g + 1) * GROUP, :] = jnp.dot(
            chosen, both, preferred_element_type=F32
        ).astype(BF)


def dispatch(ids, hidden, gain, grad):
    return pl.pallas_call(
        dispatch_kernel,
        out_shape=pltpu.VMEM((ROWS, D), BF),
        in_specs=whole(4),
        out_specs=pl.BlockSpec(memory_space=VMEM),
        compiler_params=params(),
        name="dispatch",
    )(ids, hidden, gain, grad)


def lanes(n):
    c, x = n // X, n % X
    return (x * C + c) * 256


def sort_kernel(to_sorted_ref, rows_ref, out_ref):
    for g in range(GROUPS):
        block = jnp.dot(
            to_sorted_ref[...],
            rows_ref[g * GROUP : (g + 1) * GROUP, :],
            preferred_element_type=F32,
        ).astype(BF)
        for k in range(4):
            for n in range(8):
                at = lanes(n)
                out_ref[k, g * KIND : (g + 1) * KIND, n * 256 : (n + 1) * 256] = block[
                    k * KIND : (k + 1) * KIND, at : at + 256
                ]


def sort_rows(to_sorted, rows):
    return pl.pallas_call(
        sort_kernel,
        out_shape=pltpu.VMEM((4, SLOTS, D), BF),
        in_specs=whole(2),
        out_specs=pl.BlockSpec(memory_space=VMEM),
        compiler_params=params(),
        name="sort_rows",
    )(to_sorted, rows)


def expert_kernel(rows_ref, to_natural_ref, w_ref, out_ref, in_mats, down_mat, sems):
    copies = []
    for b in range(B):
        mine = []
        for h in range(H):
            for q in range(A):
                z = (h * B + b) * A + q
                for m in range(2):
                    for f in range(3):
                        mine.append(
                            pltpu.make_async_copy(
                                w_ref.at[z, :, m, pl.ds(f * 32, 32), :],
                                in_mats.at[b, m, :, h, q, :, pl.ds(f * 128, 128)],
                                sems.at[b],
                            )
                        )
                mine.append(
                    pltpu.make_async_copy(
                        w_ref.at[z, :, 2, :, :],
                        down_mat.at[b, :, h, pl.ds(q * 96, 96), :],
                        sems.at[b],
                    )
                )
        copies.append(mine)
    for mine in copies:
        for c in mine:
            c.start()
    inner, d_gate, d_up = [], [], []
    for b in range(B):
        for c in copies[b]:
            c.wait()
        rows = rows_ref[b]
        gate_pre = jnp.dot(rows, in_mats[b, 0].reshape(D, FW), preferred_element_type=F32)
        up_pre = jnp.dot(rows, in_mats[b, 1].reshape(D, FW), preferred_element_type=F32)
        back = jnp.zeros((SLOTS, FW), F32)
        for k in range(8):
            chunk = jnp.concatenate([down_mat[b, k, 0], down_mat[b, k, 1]], axis=1)
            back = back + lax.dot_general(
                rows_ref[2 + b, :, k * 256 : (k + 1) * 256],
                chunk,
                (((1,), (1,)), ((), ())),
                preferred_element_type=F32,
            )
        s = jax.nn.sigmoid(gate_pre)
        silu = gate_pre * s
        inner.append((silu * up_pre).astype(BF))
        d_gate.append((back * up_pre * s * (1.0 + gate_pre * (1.0 - s))).astype(BF))
        d_up.append((back * silu).astype(BF))
    for k in range(8):
        parts = []
        for b in range(B):
            chunk = jnp.concatenate([down_mat[b, k, 0], down_mat[b, k, 1]], axis=1)
            parts.append(jnp.dot(inner[b], chunk, preferred_element_type=F32).astype(BF))
        for b in range(B):
            total = lax.dot_general(
                d_gate[b],
                in_mats[b, 0, k].reshape(256, FW),
                (((1,), (1,)), ((), ())),
                preferred_element_type=F32,
            ) + lax.dot_general(
                d_up[b],
                in_mats[b, 1, k].reshape(256, FW),
                (((1,), (1,)), ((), ())),
                preferred_element_type=F32,
            )
            parts.append(total.astype(BF))
        for g in range(GROUPS):
            block = jnp.concatenate([p[g * KIND : (g + 1) * KIND] for p in parts], axis=0)
            out_ref[g * GROUP : (g + 1) * GROUP, lanes(k) : lanes(k) + 256] = jnp.dot(
                to_natural_ref[...], block, preferred_element_type=F32
            ).astype(BF)


def experts(rows, to_natural, weights):
    return pl.pallas_call(
        expert_kernel,
        out_shape=pltpu.VMEM((ROWS, D), BF),
        in_specs=whole(2) + [pl.BlockSpec(memory_space=pltpu.HBM)],
        out_specs=pl.BlockSpec(memory_space=VMEM),
        scratch_shapes=[
            VMEM((B, 2, 8, H, A, 32, FW), BF),
            VMEM((B, 8, H, FW, 128), BF),
            pltpu.SemaphoreType.DMA((B,)),
        ],
        compiler_params=params(54),
        name="experts",
    )(rows, to_natural, weights)


def combine_kernel(ids_ref, codes_ref, ret_ref, hidden_ref, gain_ref, grad_ref, out_ref, gin_ref):
    r0, r1 = route_rows(ids_ref[0:1, :], ids_ref[1:2, :])
    codes = codes_ref[...].astype(F32)
    weights = codes / (codes[0:1, :] + codes[1:2, :])
    lines = jnp.concatenate(
        [r0.astype(F32), r1.astype(F32), weights, jnp.zeros((TOK - 4, TOK), F32)], axis=0
    )
    columns = jnp.transpose(lines)
    c0, c1 = columns[:, 0:1].astype(I32), columns[:, 1:2].astype(I32)
    w0, w1 = columns[:, 2:3], columns[:, 3:4]
    at = lax.broadcasted_iota(I32, (TOK, ROWS), 1)
    one, zero = jnp.ones((TOK, ROWS), F32), jnp.zeros((TOK, ROWS), F32)
    chosen = jnp.concatenate(
        [
            jnp.where(at == c + shift, one, zero).astype(BF)
            for shift in (0, 2 * CAP)
            for c in (c0, c1)
        ],
        axis=0,
    )
    picked = jnp.dot(chosen, ret_ref[...], preferred_element_type=F32)
    mixture = picked[0:TOK] * w0 + picked[TOK : 2 * TOK] * w1
    grad_normed = picked[2 * TOK : 3 * TOK] * w0 + picked[3 * TOK :] * w1
    hidden = hidden_ref[...].astype(F32)
    row_scale = row_scale_of(hidden)
    out_ref[...] = (hidden + mixture).astype(BF)
    scaled = gain_ref[...] * grad_normed
    inner_mean = jnp.mean(scaled * hidden, axis=1, keepdims=True)
    gin_ref[...] = (
        grad_ref[...].astype(F32)
        + row_scale * scaled
        - hidden * ((row_scale * row_scale * row_scale) * inner_mean)
    ).astype(BF)


def combine(ids, codes, returned, hidden, gain, grad):
    shape = jax.ShapeDtypeStruct((TOK, D), BF)
    return pl.pallas_call(
        combine_kernel,
        out_shape=(shape, shape),
        in_specs=whole(6),
        out_specs=tuple(whole(2)),
        compiler_params=params(),
        name="combine",
    )(ids, codes, returned, hidden, gain, grad)


def exchange(rows):
    blocks = rows.reshape(PEERS, PER, D)
    return lax.all_to_all(blocks, ("X", "C", "Y"), 0, 0, tiled=True).reshape(ROWS, D)


def body(hidden_in, norm_gain, w_gate, w_up, w_down, expert_ids, gate_codes, out_grad):
    gain = norm_gain.reshape(1, D)
    ids, codes = expert_ids.T, gate_codes.T
    to_natural = sort_matrix()
    pieces = place(send_home(split_weights(w_gate, w_up, w_down)))
    pieces = lax.all_to_all(pieces, "C", 0, 0, tiled=True).reshape(C * X, 3, 96, 128)
    weights = lax.all_gather(pieces, ("H", "B", "A"), axis=0, tiled=False)
    arrived = exchange(dispatch(ids, hidden_in, gain, out_grad))
    rows = sort_rows(jnp.asarray(to_natural.T, BF), arrived)
    rows = pltpu.with_memory_space_constraint(rows, VMEM)
    results = experts(rows, jnp.asarray(to_natural, BF), weights)
    returned = exchange(results)
    return combine(ids, codes, returned, hidden_in, gain, out_grad)


def solution(mesh):
    fine = Mesh(mesh.devices.reshape(X, C, H, B, A, Y), ("X", "C", "H", "B", "A", "Y"))
    tokens = P(("X", "C", "H", "B", "A", "Y"), None)
    owner, feature = ("B", "A", "Y"), ("X", "C", "H")
    in_specs = (
        tokens,
        P(),
        P(owner, feature, None),
        P(owner, feature, None),
        P(owner, None, feature),
        tokens,
        tokens,
        tokens,
    )
    return jax.shard_map(
        body, mesh=fine, in_specs=in_specs, out_specs=(tokens, tokens), check_vma=False
    )
```

```python
import numpy as np
import jax
import jax.numpy as jnp
from jax import lax
from jax.experimental import pallas as pl
from jax.experimental.pallas import tpu as pltpu
from jax.sharding import Mesh, PartitionSpec as P

epsilon = 1e-06
BF = jnp.bfloat16
F32 = jnp.float32
I32 = jnp.int32
VMEM = pltpu.VMEM
MIB = 1024 * 1024

X, C, H, B, A, Y = 4, 2, 2, 2, 4, 4
PEERS = X * C * Y
TOK, D, FW, CAP = 128, 2048, 384, 6
PER = 4 * CAP
ROWS = PEERS * PER
GROUPS = 4
GROUP = ROWS // GROUPS
KIND = GROUP // 4
SLOTS = GROUPS * KIND


def sort_matrix():
    natural = np.arange(GROUP)
    place = (natural % PER) // CAP * KIND + natural // PER * CAP + natural % CAP
    to_natural = np.zeros((GROUP, GROUP), np.float32)
    to_natural[natural, place] = 1.0
    return to_natural


def whole(n):
    return [pl.BlockSpec(memory_space=VMEM)] * n


def params(mib=24):
    return pltpu.CompilerParams(vmem_limit_bytes=mib * MIB)


def split_kernel(gate_ref, up_ref, down_ref, *out_refs):
    x = lax.axis_index("X")
    for r in range(X):
        q = (x + r) & 3
        for e in range(2):
            for m, ref in enumerate((gate_ref, up_ref)):
                for f in range(3):
                    out_refs[r][e, m, f * 32 : (f + 1) * 32, :] = ref[
                        e, pl.ds(pl.multiple_of(q * 32, 32), 32), f * 128 : (f + 1) * 128
                    ]
            out_refs[r][e, 2] = down_ref[e, pl.ds(pl.multiple_of(q * 96, 32), 96), :]


def split_weights(w_gate, w_up, w_down):
    return pl.pallas_call(
        split_kernel,
        out_shape=(jax.ShapeDtypeStruct((2, 3, 96, 128), BF),) * X,
        in_specs=whole(3),
        out_specs=tuple(whole(X)),
        compiler_params=params(),
        name="split_weights",
    )(w_gate, w_up, w_down)


def send_home(pieces):
    moved = []
    for r in range(X):
        pairs = [(x * A + a, a * A + (x + r) % X) for x in range(X) for a in range(A)]
        moved.append(lax.ppermute(pieces[r], ("X", "A"), pairs))
    return moved


def place_kernel(*refs):
    keep_ref, give_ref, sem = refs[X:]
    a, c = lax.axis_index("A"), lax.axis_index("C")
    copies = []
    for r in range(X):
        at = (a - r) & 3
        copies.append(pltpu.make_async_copy(refs[r].at[c], keep_ref.at[at], sem))
        copies.append(pltpu.make_async_copy(refs[r].at[1 - c], give_ref.at[at], sem))
    for copy in copies:
        copy.start()
    for copy in copies:
        copy.wait()


def place(pieces):
    return pl.pallas_call(
        place_kernel,
        out_shape=(pltpu.VMEM((X, 3, 96, 128), BF),) * 2,
        in_specs=[pl.BlockSpec(memory_space=pl.ANY)] * X,
        out_specs=tuple(whole(2)),
        scratch_shapes=[pltpu.SemaphoreType.DMA],
        compiler_params=params(),
        name="place",
    )(*pieces)


Z = H * B * A
UP = [(z, (z + 1) % Z) for z in range(Z)]
DOWN = [(z, (z - 1) % Z) for z in range(Z)]


def around(halves):
    found = [[half] + [None] * (Z - 1) for half in halves]
    axes = ("H", "B", "A")
    for k in range(1, Z // 2 + 1):
        for i in range(2):
            found[i][k] = lax.ppermute(found[i][k - 1], axes, UP)
            if k < Z // 2:
                found[i][Z - k] = lax.ppermute(found[i][(Z - k + 1) % Z], axes, DOWN)
    return [pltpu.with_memory_space_constraint(f, pltpu.HBM) for f in found[0] + found[1]]


def route_rows(ids0, ids1):
    labels = lax.broadcasted_iota(I32, (64, TOK), 0)
    m0, m1 = labels == ids0, labels == ids1
    one, zero = jnp.ones((64, TOK), F32), jnp.zeros((64, TOK), F32)
    both = (jnp.where(m0, one, zero) + jnp.where(m1, one, zero)).astype(BF)
    earlier = jnp.where(
        lax.broadcasted_iota(I32, (TOK, TOK), 0) < lax.broadcasted_iota(I32, (TOK, TOK), 1),
        jnp.ones((TOK, TOK), F32),
        jnp.zeros((TOK, TOK), F32),
    ).astype(BF)
    before = jnp.dot(both, earlier, preferred_element_type=F32)

    def row(ids, mask):
        position = jnp.sum(jnp.where(mask, before, zero), axis=0, keepdims=True).astype(I32)
        x, b = (ids >> 3) & 3, ids >> 5
        y, c = (ids >> 1) & 3, ids & 1
        return ((x * C + c) * Y + y) * PER + b * CAP + position

    return row(ids0, m0), row(ids1, m1)


def row_scale_of(hidden):
    return lax.rsqrt(jnp.mean(hidden * hidden, axis=1, keepdims=True) + epsilon)


def dispatch_kernel(ids_ref, hidden_ref, gain_ref, grad_ref, out_ref):
    hidden = hidden_ref[...].astype(F32)
    normed = (hidden * row_scale_of(hidden) * gain_ref[...]).astype(BF)
    both = jnp.concatenate([normed, grad_ref[...]], axis=0)
    r0, r1 = route_rows(ids_ref[0:1, :], ids_ref[1:2, :])
    one, zero = jnp.ones((GROUP, TOK), F32), jnp.zeros((GROUP, TOK), F32)
    for g in range(GROUPS):
        at = lax.broadcasted_iota(I32, (GROUP, TOK), 0) + g * GROUP
        picks = []
        for shift in (0, 2 * CAP):
            hit = (at == r0 + shift) | (at == r1 + shift)
            picks.append(jnp.where(hit, one, zero).astype(BF))
        chosen = jnp.concatenate(picks, axis=1)
        out_ref[g * GROUP : (g + 1) * GROUP, :] = jnp.dot(
            chosen, both, preferred_element_type=F32
        ).astype(BF)


def dispatch(ids, hidden, gain, grad):
    return pl.pallas_call(
        dispatch_kernel,
        out_shape=pltpu.VMEM((ROWS, D), BF),
        in_specs=whole(4),
        out_specs=pl.BlockSpec(memory_space=VMEM),
        compiler_params=params(),
        name="dispatch",
    )(ids, hidden, gain, grad)


def lanes(n):
    c, x = n // X, n % X
    return (x * C + c) * 256


def sort_kernel(to_sorted_ref, rows_ref, out_ref):
    for g in range(GROUPS):
        block = jnp.dot(
            to_sorted_ref[...],
            rows_ref[g * GROUP : (g + 1) * GROUP, :],
            preferred_element_type=F32,
        ).astype(BF)
        for k in range(4):
            for n in range(8):
                at = lanes(n)
                out_ref[k, g * KIND : (g + 1) * KIND, n * 256 : (n + 1) * 256] = block[
                    k * KIND : (k + 1) * KIND, at : at + 256
                ]


def sort_rows(to_sorted, rows):
    return pl.pallas_call(
        sort_kernel,
        out_shape=pltpu.VMEM((4, SLOTS, D), BF),
        in_specs=whole(2),
        out_specs=pl.BlockSpec(memory_space=VMEM),
        compiler_params=params(),
        name="sort_rows",
    )(to_sorted, rows)


def expert_kernel(rows_ref, to_natural_ref, *refs):
    pieces, (out_ref, in_mats, down_mat, sem) = refs[: 2 * Z], refs[2 * Z :]
    me = (lax.axis_index("H") * B + lax.axis_index("B")) * A + lax.axis_index("A")
    core = lax.axis_index("C")
    copies = []
    for i in range(2):
        c = core if i == 0 else 1 - core
        for k in range(Z):
            z = (me - k) & (Z - 1)
            h, b, q = z >> 3, (z >> 2) & 1, z & 3
            ref = pieces[i * Z + k]
            for m in range(2):
                for f in range(3):
                    copies.append(
                        pltpu.make_async_copy(
                            ref.at[:, m, pl.ds(f * 32, 32), :],
                            in_mats.at[b, m, c, :, h, q, :, pl.ds(f * 128, 128)],
                            sem,
                        )
                    )
            copies.append(pltpu.make_async_copy(ref.at[:, 2], down_mat.at[b, c, :, h, q], sem))
    for copy in copies:
        copy.start()
    for copy in copies:
        copy.wait()

    def down_chunk(b, k):
        c, x = k // X, k % X
        return jnp.concatenate(
            [down_mat[b, c, x, h].reshape(FW, 128) for h in range(H)], axis=1
        )

    inner, d_gate, d_up = [], [], []
    for b in range(B):
        rows = rows_ref[b]
        gate_pre = jnp.dot(rows, in_mats[b, 0].reshape(D, FW), preferred_element_type=F32)
        up_pre = jnp.dot(rows, in_mats[b, 1].reshape(D, FW), preferred_element_type=F32)
        back = jnp.zeros((SLOTS, FW), F32)
        for k in range(8):
            chunk = down_chunk(b, k)
            back = back + lax.dot_general(
                rows_ref[2 + b, :, k * 256 : (k + 1) * 256],
                chunk,
                (((1,), (1,)), ((), ())),
                preferred_element_type=F32,
            )
        s = jax.nn.sigmoid(gate_pre)
        silu = gate_pre * s
        inner.append((silu * up_pre).astype(BF))
        d_gate.append((back * up_pre * s * (1.0 + gate_pre * (1.0 - s))).astype(BF))
        d_up.append((back * silu).astype(BF))
    for k in range(8):
        parts = []
        for b in range(B):
            chunk = down_chunk(b, k)
            parts.append(jnp.dot(inner[b], chunk, preferred_element_type=F32).astype(BF))
        for b in range(B):
            total = lax.dot_general(
                d_gate[b],
                in_mats[b, 0, k // X, k % X].reshape(256, FW),
                (((1,), (1,)), ((), ())),
                preferred_element_type=F32,
            ) + lax.dot_general(
                d_up[b],
                in_mats[b, 1, k // X, k % X].reshape(256, FW),
                (((1,), (1,)), ((), ())),
                preferred_element_type=F32,
            )
            parts.append(total.astype(BF))
        for g in range(GROUPS):
            block = jnp.concatenate([p[g * KIND : (g + 1) * KIND] for p in parts], axis=0)
            out_ref[g * GROUP : (g + 1) * GROUP, lanes(k) : lanes(k) + 256] = jnp.dot(
                to_natural_ref[...], block, preferred_element_type=F32
            ).astype(BF)


def experts(rows, to_natural, weights):
    return pl.pallas_call(
        expert_kernel,
        out_shape=pltpu.VMEM((ROWS, D), BF),
        in_specs=whole(2) + [pl.BlockSpec(memory_space=pl.ANY)] * (2 * Z),
        out_specs=pl.BlockSpec(memory_space=VMEM),
        scratch_shapes=[
            VMEM((B, 2, C, X, H, A, 32, FW), BF),
            VMEM((B, C, X, H, A, 96, 128), BF),
            pltpu.SemaphoreType.DMA,
        ],
        compiler_params=params(36),
        name="experts",
    )(rows, to_natural, *weights)


def combine_kernel(ids_ref, codes_ref, ret_ref, hidden_ref, gain_ref, grad_ref, out_ref, gin_ref):
    r0, r1 = route_rows(ids_ref[0:1, :], ids_ref[1:2, :])
    codes = codes_ref[...].astype(F32)
    weights = codes / (codes[0:1, :] + codes[1:2, :])
    lines = jnp.concatenate(
        [r0.astype(F32), r1.astype(F32), weights, jnp.zeros((TOK - 4, TOK), F32)], axis=0
    )
    columns = jnp.transpose(lines)
    c0, c1 = columns[:, 0:1].astype(I32), columns[:, 1:2].astype(I32)
    w0, w1 = columns[:, 2:3], columns[:, 3:4]
    at = lax.broadcasted_iota(I32, (TOK, ROWS), 1)
    one, zero = jnp.ones((TOK, ROWS), F32), jnp.zeros((TOK, ROWS), F32)
    chosen = jnp.concatenate(
        [
            jnp.where(at == c + shift, one, zero).astype(BF)
            for shift in (0, 2 * CAP)
            for c in (c0, c1)
        ],
        axis=0,
    )
    picked = jnp.dot(chosen, ret_ref[...], preferred_element_type=F32)
    mixture = picked[0:TOK] * w0 + picked[TOK : 2 * TOK] * w1
    grad_normed = picked[2 * TOK : 3 * TOK] * w0 + picked[3 * TOK :] * w1
    hidden = hidden_ref[...].astype(F32)
    row_scale = row_scale_of(hidden)
    out_ref[...] = (hidden + mixture).astype(BF)
    scaled = gain_ref[...] * grad_normed
    inner_mean = jnp.mean(scaled * hidden, axis=1, keepdims=True)
    gin_ref[...] = (
        grad_ref[...].astype(F32)
        + row_scale * scaled
        - hidden * ((row_scale * row_scale * row_scale) * inner_mean)
    ).astype(BF)


def combine(ids, codes, returned, hidden, gain, grad):
    shape = jax.ShapeDtypeStruct((TOK, D), BF)
    return pl.pallas_call(
        combine_kernel,
        out_shape=(shape, shape),
        in_specs=whole(6),
        out_specs=tuple(whole(2)),
        compiler_params=params(),
        name="combine",
    )(ids, codes, returned, hidden, gain, grad)


def exchange(rows):
    blocks = rows.reshape(PEERS, PER, D)
    return lax.all_to_all(blocks, ("X", "C", "Y"), 0, 0, tiled=True).reshape(ROWS, D)


def body(hidden_in, norm_gain, w_gate, w_up, w_down, expert_ids, gate_codes, out_grad):
    gain = norm_gain.reshape(1, D)
    ids, codes = expert_ids.T, gate_codes.T
    to_natural = sort_matrix()
    keep, give = place(send_home(split_weights(w_gate, w_up, w_down)))
    weights = around((keep, lax.ppermute(give, "C", [(0, 1), (1, 0)])))
    hidden_late, _ = lax.optimization_barrier(
        (hidden_in, [weights[k] for k in (1, Z - 1, Z + 1, 2 * Z - 1)])
    )
    arrived = exchange(dispatch(ids, hidden_late, gain, out_grad))
    rows = sort_rows(jnp.asarray(to_natural.T, BF), arrived)
    rows = pltpu.with_memory_space_constraint(rows, VMEM)
    results = experts(rows, jnp.asarray(to_natural, BF), weights)
    returned = exchange(results)
    return combine(ids, codes, returned, hidden_in, gain, out_grad)


def solution(mesh):
    fine = Mesh(mesh.devices.reshape(X, C, H, B, A, Y), ("X", "C", "H", "B", "A", "Y"))
    tokens = P(("X", "C", "H", "B", "A", "Y"), None)
    owner, feature = ("B", "A", "Y"), ("X", "C", "H")
    in_specs = (
        tokens,
        P(),
        P(owner, feature, None),
        P(owner, feature, None),
        P(owner, None, feature),
        tokens,
        tokens,
        tokens,
    )
    return jax.shard_map(
        body, mesh=fine, in_specs=in_specs, out_specs=(tokens, tokens), check_vma=False
    )
```

```python
import numpy as np
import jax
import jax.numpy as jnp
from jax import lax
from jax.experimental import pallas as pl
from jax.experimental.pallas import tpu as pltpu
from jax.sharding import Mesh, PartitionSpec as P

epsilon = 1e-06
BF = jnp.bfloat16
F32 = jnp.float32
I32 = jnp.int32
VMEM = pltpu.VMEM
MIB = 1024 * 1024

X, C, H, B, A, Y = 4, 2, 2, 2, 4, 4
PEERS = X * C * Y
TOK, D, FW, CAP = 128, 2048, 384, 6
PER = 4 * CAP
ROWS = PEERS * PER
GROUPS = 4
GROUP = ROWS // GROUPS
KIND = GROUP // 4
SLOTS = GROUPS * KIND


def sort_matrix():
    natural = np.arange(GROUP)
    place = (natural % PER) // CAP * KIND + natural // PER * CAP + natural % CAP
    to_natural = np.zeros((GROUP, GROUP), np.float32)
    to_natural[natural, place] = 1.0
    return to_natural


def whole(n):
    return [pl.BlockSpec(memory_space=VMEM)] * n


def params(mib=24):
    return pltpu.CompilerParams(vmem_limit_bytes=mib * MIB)


def split_kernel(gate_ref, up_ref, down_ref, *refs):
    out_refs, sem = refs[:X], refs[X]
    x = lax.axis_index("X")
    copies = []
    for r in range(X):
        q = (x + r) & 3
        rows = pl.ds(pl.multiple_of(q * 32, 32), 32)
        for m, ref in enumerate((gate_ref, up_ref)):
            for f in range(3):
                copies.append(
                    pltpu.make_async_copy(
                        ref.at[:, rows, pl.ds(f * 128, 128)],
                        out_refs[r].at[:, m, pl.ds(f * 32, 32), :],
                        sem,
                    )
                )
        rows = pl.ds(pl.multiple_of(q * 96, 32), 96)
        copies.append(
            pltpu.make_async_copy(down_ref.at[:, rows, :], out_refs[r].at[:, 2, :, :], sem)
        )
    for copy in copies:
        copy.start()
    for copy in copies:
        copy.wait()


def split_weights(*mats):
    mats = [pltpu.with_memory_space_constraint(mat, pltpu.HBM) for mat in mats]
    return pl.pallas_call(
        split_kernel,
        out_shape=(pltpu.VMEM((2, 3, 96, 128), BF),) * X,
        in_specs=[pl.BlockSpec(memory_space=pltpu.HBM)] * 3,
        out_specs=tuple(whole(X)),
        scratch_shapes=[pltpu.SemaphoreType.DMA],
        compiler_params=params(),
        name="split_weights",
    )(*mats)


def send_home(pieces):
    moved = []
    for r in range(X):
        pairs = [(x * A + a, a * A + (x + r) % X) for x in range(X) for a in range(A)]
        moved.append(lax.ppermute(pieces[r], ("X", "A"), pairs))
    return moved


def place_kernel(*refs):
    keep_ref, give_ref, sem = refs[X:]
    a, c = lax.axis_index("A"), lax.axis_index("C")
    copies = []
    for r in range(X):
        at = (a - r) & 3
        copies.append(pltpu.make_async_copy(refs[r].at[c], keep_ref.at[at], sem))
        copies.append(pltpu.make_async_copy(refs[r].at[1 - c], give_ref.at[at], sem))
    for copy in copies:
        copy.start()
    for copy in copies:
        copy.wait()


def place(pieces):
    return pl.pallas_call(
        place_kernel,
        out_shape=(pltpu.VMEM((X, 3, 96, 128), BF),) * 2,
        in_specs=[pl.BlockSpec(memory_space=pl.ANY)] * X,
        out_specs=tuple(whole(2)),
        scratch_shapes=[pltpu.SemaphoreType.DMA],
        compiler_params=params(),
        name="place",
    )(*pieces)


Z = H * B * A
UP = [(z, (z + 1) % Z) for z in range(Z)]
DOWN = [(z, (z - 1) % Z) for z in range(Z)]


def around(halves):
    found = [[half] + [None] * (Z - 1) for half in halves]
    axes = ("H", "B", "A")
    for k in range(1, Z // 2 + 1):
        for i in range(2):
            found[i][k] = lax.ppermute(found[i][k - 1], axes, UP)
            if k < Z // 2:
                found[i][Z - k] = lax.ppermute(found[i][(Z - k + 1) % Z], axes, DOWN)
    return [pltpu.with_memory_space_constraint(f, pltpu.HBM) for f in found[0] + found[1]]


def route_rows(ids0, ids1):
    labels = lax.broadcasted_iota(I32, (64, TOK), 0)
    m0, m1 = labels == ids0, labels == ids1
    one, zero = jnp.ones((64, TOK), F32), jnp.zeros((64, TOK), F32)
    both = (jnp.where(m0, one, zero) + jnp.where(m1, one, zero)).astype(BF)
    earlier = jnp.where(
        lax.broadcasted_iota(I32, (TOK, TOK), 0) < lax.broadcasted_iota(I32, (TOK, TOK), 1),
        jnp.ones((TOK, TOK), F32),
        jnp.zeros((TOK, TOK), F32),
    ).astype(BF)
    before = jnp.dot(both, earlier, preferred_element_type=F32)

    def row(ids, mask):
        position = jnp.sum(jnp.where(mask, before, zero), axis=0, keepdims=True).astype(I32)
        x, b = (ids >> 3) & 3, ids >> 5
        y, c = (ids >> 1) & 3, ids & 1
        return ((x * C + c) * Y + y) * PER + b * CAP + position

    return row(ids0, m0), row(ids1, m1)


def row_scale_of(hidden):
    return lax.rsqrt(jnp.mean(hidden * hidden, axis=1, keepdims=True) + epsilon)


def dispatch_kernel(ids_ref, hidden_ref, gain_ref, grad_ref, out_ref):
    hidden = hidden_ref[...].astype(F32)
    normed = (hidden * row_scale_of(hidden) * gain_ref[...]).astype(BF)
    both = jnp.concatenate([normed, grad_ref[...]], axis=0)
    r0, r1 = route_rows(ids_ref[0:1, :], ids_ref[1:2, :])
    one, zero = jnp.ones((GROUP, TOK), F32), jnp.zeros((GROUP, TOK), F32)
    for g in range(GROUPS):
        at = lax.broadcasted_iota(I32, (GROUP, TOK), 0) + g * GROUP
        picks = []
        for shift in (0, 2 * CAP):
            hit = (at == r0 + shift) | (at == r1 + shift)
            picks.append(jnp.where(hit, one, zero).astype(BF))
        chosen = jnp.concatenate(picks, axis=1)
        out_ref[g * GROUP : (g + 1) * GROUP, :] = jnp.dot(
            chosen, both, preferred_element_type=F32
        ).astype(BF)


def dispatch(ids, hidden, gain, grad):
    return pl.pallas_call(
        dispatch_kernel,
        out_shape=pltpu.VMEM((ROWS, D), BF),
        in_specs=whole(4),
        out_specs=pl.BlockSpec(memory_space=VMEM),
        compiler_params=params(),
        name="dispatch",
    )(ids, hidden, gain, grad)


def lanes(n):
    c, x = n // X, n % X
    return (x * C + c) * 256


def sort_kernel(to_sorted_ref, rows_ref, out_ref):
    for g in range(GROUPS):
        block = jnp.dot(
            to_sorted_ref[...],
            rows_ref[g * GROUP : (g + 1) * GROUP, :],
            preferred_element_type=F32,
        ).astype(BF)
        for k in range(4):
            for n in range(8):
                at = lanes(n)
                out_ref[k, g * KIND : (g + 1) * KIND, n * 256 : (n + 1) * 256] = block[
                    k * KIND : (k + 1) * KIND, at : at + 256
                ]


def sort_rows(to_sorted, rows):
    return pl.pallas_call(
        sort_kernel,
        out_shape=pltpu.VMEM((4, SLOTS, D), BF),
        in_specs=whole(2),
        out_specs=pl.BlockSpec(memory_space=VMEM),
        compiler_params=params(),
        name="sort_rows",
    )(to_sorted, rows)


def expert_kernel(rows_ref, to_natural_ref, *refs):
    pieces, (out_ref, in_mats, down_mat, sem) = refs[: 2 * Z], refs[2 * Z :]
    me = (lax.axis_index("H") * B + lax.axis_index("B")) * A + lax.axis_index("A")
    core = lax.axis_index("C")
    copies = []
    for i in range(2):
        c = core if i == 0 else 1 - core
        for k in range(Z):
            z = (me - k) & (Z - 1)
            h, b, q = z >> 3, (z >> 2) & 1, z & 3
            ref = pieces[i * Z + k]
            for m in range(2):
                for f in range(3):
                    copies.append(
                        pltpu.make_async_copy(
                            ref.at[:, m, pl.ds(f * 32, 32), :],
                            in_mats.at[b, m, c, :, h, q, :, pl.ds(f * 128, 128)],
                            sem,
                        )
                    )
            copies.append(pltpu.make_async_copy(ref.at[:, 2], down_mat.at[b, c, :, h, q], sem))
    for copy in copies:
        copy.start()
    for copy in copies:
        copy.wait()

    def down_chunk(b, k):
        c, x = k // X, k % X
        return jnp.concatenate(
            [down_mat[b, c, x, h].reshape(FW, 128) for h in range(H)], axis=1
        )

    inner, d_gate, d_up = [], [], []
    for b in range(B):
        rows = rows_ref[b]
        gate_pre = jnp.dot(rows, in_mats[b, 0].reshape(D, FW), preferred_element_type=F32)
        up_pre = jnp.dot(rows, in_mats[b, 1].reshape(D, FW), preferred_element_type=F32)
        back = jnp.zeros((SLOTS, FW), F32)
        for k in range(8):
            chunk = down_chunk(b, k)
            back = back + lax.dot_general(
                rows_ref[2 + b, :, k * 256 : (k + 1) * 256],
                chunk,
                (((1,), (1,)), ((), ())),
                preferred_element_type=F32,
            )
        s = jax.nn.sigmoid(gate_pre)
        silu = gate_pre * s
        inner.append((silu * up_pre).astype(BF))
        d_gate.append((back * up_pre * s * (1.0 + gate_pre * (1.0 - s))).astype(BF))
        d_up.append((back * silu).astype(BF))
    for k in range(8):
        parts = []
        for b in range(B):
            chunk = down_chunk(b, k)
            parts.append(jnp.dot(inner[b], chunk, preferred_element_type=F32).astype(BF))
        for b in range(B):
            total = lax.dot_general(
                d_gate[b],
                in_mats[b, 0, k // X, k % X].reshape(256, FW),
                (((1,), (1,)), ((), ())),
                preferred_element_type=F32,
            ) + lax.dot_general(
                d_up[b],
                in_mats[b, 1, k // X, k % X].reshape(256, FW),
                (((1,), (1,)), ((), ())),
                preferred_element_type=F32,
            )
            parts.append(total.astype(BF))
        for g in range(GROUPS):
            block = jnp.concatenate([p[g * KIND : (g + 1) * KIND] for p in parts], axis=0)
            out_ref[g * GROUP : (g + 1) * GROUP, lanes(k) : lanes(k) + 256] = jnp.dot(
                to_natural_ref[...], block, preferred_element_type=F32
            ).astype(BF)


def experts(rows, to_natural, weights):
    return pl.pallas_call(
        expert_kernel,
        out_shape=pltpu.VMEM((ROWS, D), BF),
        in_specs=whole(2) + [pl.BlockSpec(memory_space=pl.ANY)] * (2 * Z),
        out_specs=pl.BlockSpec(memory_space=VMEM),
        scratch_shapes=[
            VMEM((B, 2, C, X, H, A, 32, FW), BF),
            VMEM((B, C, X, H, A, 96, 128), BF),
            pltpu.SemaphoreType.DMA,
        ],
        compiler_params=params(36),
        name="experts",
    )(rows, to_natural, *weights)


def combine_kernel(ids_ref, codes_ref, ret_ref, hidden_ref, gain_ref, grad_ref, out_ref, gin_ref):
    r0, r1 = route_rows(ids_ref[0:1, :], ids_ref[1:2, :])
    codes = codes_ref[...].astype(F32)
    weights = codes / (codes[0:1, :] + codes[1:2, :])
    lines = jnp.concatenate(
        [r0.astype(F32), r1.astype(F32), weights, jnp.zeros((TOK - 4, TOK), F32)], axis=0
    )
    columns = jnp.transpose(lines)
    c0, c1 = columns[:, 0:1].astype(I32), columns[:, 1:2].astype(I32)
    w0, w1 = columns[:, 2:3], columns[:, 3:4]
    at = lax.broadcasted_iota(I32, (TOK, ROWS), 1)
    one, zero = jnp.ones((TOK, ROWS), F32), jnp.zeros((TOK, ROWS), F32)
    chosen = jnp.concatenate(
        [
            jnp.where(at == c + shift, one, zero).astype(BF)
            for shift in (0, 2 * CAP)
            for c in (c0, c1)
        ],
        axis=0,
    )
    picked = jnp.dot(chosen, ret_ref[...], preferred_element_type=F32)
    mixture = picked[0:TOK] * w0 + picked[TOK : 2 * TOK] * w1
    grad_normed = picked[2 * TOK : 3 * TOK] * w0 + picked[3 * TOK :] * w1
    hidden = hidden_ref[...].astype(F32)
    row_scale = row_scale_of(hidden)
    out_ref[...] = (hidden + mixture).astype(BF)
    scaled = gain_ref[...] * grad_normed
    inner_mean = jnp.mean(scaled * hidden, axis=1, keepdims=True)
    gin_ref[...] = (
        grad_ref[...].astype(F32)
        + row_scale * scaled
        - hidden * ((row_scale * row_scale * row_scale) * inner_mean)
    ).astype(BF)


def combine(ids, codes, returned, hidden, gain, grad):
    shape = jax.ShapeDtypeStruct((TOK, D), BF)
    return pl.pallas_call(
        combine_kernel,
        out_shape=(shape, shape),
        in_specs=whole(6),
        out_specs=tuple(whole(2)),
        compiler_params=params(),
        name="combine",
    )(ids, codes, returned, hidden, gain, grad)


def exchange(rows):
    blocks = rows.reshape(PEERS, PER, D)
    return lax.all_to_all(blocks, ("X", "C", "Y"), 0, 0, tiled=True).reshape(ROWS, D)


def body(hidden_in, norm_gain, w_gate, w_up, w_down, expert_ids, gate_codes, out_grad):
    gain = norm_gain.reshape(1, D)
    ids, codes = expert_ids.T, gate_codes.T
    to_natural = sort_matrix()
    keep, give = place(send_home(split_weights(w_gate, w_up, w_down)))
    weights = around((keep, lax.ppermute(give, "C", [(0, 1), (1, 0)])))
    sent = dispatch(ids, hidden_in, gain, out_grad)
    arrived = exchange(sent)
    rows = sort_rows(jnp.asarray(to_natural.T, BF), arrived)
    rows = pltpu.with_memory_space_constraint(rows, VMEM)
    results = experts(rows, jnp.asarray(to_natural, BF), weights)
    returned = exchange(results)
    return combine(ids, codes, returned, hidden_in, gain, out_grad)


def solution(mesh):
    fine = Mesh(mesh.devices.reshape(X, C, H, B, A, Y), ("X", "C", "H", "B", "A", "Y"))
    tokens = P(("X", "C", "H", "B", "A", "Y"), None)
    owner, feature = ("B", "A", "Y"), ("X", "C", "H")
    in_specs = (
        tokens,
        P(),
        P(owner, feature, None),
        P(owner, feature, None),
        P(owner, None, feature),
        tokens,
        tokens,
        tokens,
    )
    return jax.shard_map(
        body, mesh=fine, in_specs=in_specs, out_specs=(tokens, tokens), check_vma=False
    )
```

```python
import numpy as np
import jax
import jax.numpy as jnp
from jax import lax
from jax.experimental import pallas as pl
from jax.experimental.pallas import tpu as pltpu
from jax.sharding import Mesh, PartitionSpec as P

epsilon = 1e-06
BF = jnp.bfloat16
F32 = jnp.float32
I32 = jnp.int32
VMEM = pltpu.VMEM
MIB = 1024 * 1024

X, C, H, B, A, Y = 4, 2, 2, 2, 4, 4
PEERS = X * C * Y
TOK, D, FW, CAP = 128, 2048, 384, 6
PER = 4 * CAP
ROWS = PEERS * PER
GROUPS = 4
GROUP = ROWS // GROUPS
KIND = GROUP // 4
SLOTS = GROUPS * KIND


def sort_matrix():
    natural = np.arange(GROUP)
    place = (natural % PER) // CAP * KIND + natural // PER * CAP + natural % CAP
    to_natural = np.zeros((GROUP, GROUP), np.float32)
    to_natural[natural, place] = 1.0
    return to_natural


def whole(n):
    return [pl.BlockSpec(memory_space=VMEM)] * n


def params(mib=24):
    return pltpu.CompilerParams(vmem_limit_bytes=mib * MIB)


def split_kernel(gate_ref, up_ref, down_ref, *refs):
    out_refs, sem = refs[:X], refs[X]
    x = lax.axis_index("X")
    copies = []
    for r in range(X):
        q = (x + r) & 3
        rows = pl.ds(pl.multiple_of(q * 32, 32), 32)
        for m, ref in enumerate((gate_ref, up_ref)):
            for f in range(3):
                copies.append(
                    pltpu.make_async_copy(
                        ref.at[:, rows, pl.ds(f * 128, 128)],
                        out_refs[r].at[:, m, pl.ds(f * 32, 32), :],
                        sem,
                    )
                )
        rows = pl.ds(pl.multiple_of(q * 96, 32), 96)
        copies.append(
            pltpu.make_async_copy(down_ref.at[:, rows, :], out_refs[r].at[:, 2, :, :], sem)
        )
    for copy in copies:
        copy.start()
    for copy in copies:
        copy.wait()


def split_weights(*mats):
    mats = [pltpu.with_memory_space_constraint(mat, pltpu.HBM) for mat in mats]
    return pl.pallas_call(
        split_kernel,
        out_shape=(pltpu.VMEM((2, 3, 96, 128), BF),) * X,
        in_specs=[pl.BlockSpec(memory_space=pltpu.HBM)] * 3,
        out_specs=tuple(whole(X)),
        scratch_shapes=[pltpu.SemaphoreType.DMA],
        compiler_params=params(),
        name="split_weights",
    )(*mats)


def send_home(pieces):
    moved = []
    for r in range(X):
        pairs = [(x * A + a, a * A + (x + r) % X) for x in range(X) for a in range(A)]
        moved.append(lax.ppermute(pieces[r], ("X", "A"), pairs))
    return moved


def place_kernel(*refs):
    out_ref, sem = refs[X:]
    a = lax.axis_index("A")
    copies = [
        pltpu.make_async_copy(refs[r], out_ref.at[:, (a - r) & 3], sem) for r in range(X)
    ]
    for copy in copies:
        copy.start()
    for copy in copies:
        copy.wait()


def place(pieces):
    return pl.pallas_call(
        place_kernel,
        out_shape=pltpu.VMEM((2, X, 3, 96, 128), BF),
        in_specs=[pl.BlockSpec(memory_space=pl.ANY)] * X,
        out_specs=pl.BlockSpec(memory_space=VMEM),
        scratch_shapes=[pltpu.SemaphoreType.DMA],
        compiler_params=params(),
        name="place",
    )(*pieces)


Z = H * B * A
UP = [(z, (z + 1) % Z) for z in range(Z)]
DOWN = [(z, (z - 1) % Z) for z in range(Z)]


def around(piece):
    axes, half = ("H", "B", "A"), Z // 2
    found = [piece] + [None] * (Z - 1)
    for k in range(1, half):
        found[k] = lax.ppermute(found[k - 1], axes, UP)
        found[Z - k] = lax.ppermute(found[(Z - k + 1) % Z], axes, DOWN)
    found[half] = lax.ppermute(found[half - 1][0], axes, UP)
    found.append(lax.ppermute(found[half + 1][1], axes, DOWN))
    return [pltpu.with_memory_space_constraint(f, pltpu.HBM) for f in found]


def route_rows(ids0, ids1):
    labels = lax.broadcasted_iota(I32, (64, TOK), 0)
    m0, m1 = labels == ids0, labels == ids1
    one, zero = jnp.ones((64, TOK), F32), jnp.zeros((64, TOK), F32)
    both = (jnp.where(m0, one, zero) + jnp.where(m1, one, zero)).astype(BF)
    earlier = jnp.where(
        lax.broadcasted_iota(I32, (TOK, TOK), 0) < lax.broadcasted_iota(I32, (TOK, TOK), 1),
        jnp.ones((TOK, TOK), F32),
        jnp.zeros((TOK, TOK), F32),
    ).astype(BF)
    before = jnp.dot(both, earlier, preferred_element_type=F32)

    def row(ids, mask):
        position = jnp.sum(jnp.where(mask, before, zero), axis=0, keepdims=True).astype(I32)
        x, b = (ids >> 3) & 3, ids >> 5
        y, c = (ids >> 1) & 3, ids & 1
        return ((x * C + c) * Y + y) * PER + b * CAP + position

    return row(ids0, m0), row(ids1, m1)


def row_scale_of(hidden):
    return lax.rsqrt(jnp.mean(hidden * hidden, axis=1, keepdims=True) + epsilon)


def dispatch_kernel(ids_ref, hidden_ref, gain_ref, grad_ref, out_ref):
    hidden = hidden_ref[...].astype(F32)
    normed = (hidden * row_scale_of(hidden) * gain_ref[...]).astype(BF)
    both = jnp.concatenate([normed, grad_ref[...]], axis=0)
    r0, r1 = route_rows(ids_ref[0:1, :], ids_ref[1:2, :])
    one, zero = jnp.ones((GROUP, TOK), F32), jnp.zeros((GROUP, TOK), F32)
    for g in range(GROUPS):
        at = lax.broadcasted_iota(I32, (GROUP, TOK), 0) + g * GROUP
        picks = []
        for shift in (0, 2 * CAP):
            hit = (at == r0 + shift) | (at == r1 + shift)
            picks.append(jnp.where(hit, one, zero).astype(BF))
        chosen = jnp.concatenate(picks, axis=1)
        out_ref[g * GROUP : (g + 1) * GROUP, :] = jnp.dot(
            chosen, both, preferred_element_type=F32
        ).astype(BF)


def dispatch(ids, hidden, gain, grad):
    return pl.pallas_call(
        dispatch_kernel,
        out_shape=pltpu.VMEM((ROWS, D), BF),
        in_specs=whole(4),
        out_specs=pl.BlockSpec(memory_space=VMEM),
        compiler_params=params(),
        name="dispatch",
    )(ids, hidden, gain, grad)


def lanes(n):
    c, x = n // X, n % X
    return (x * C + c) * 256


def sort_kernel(to_sorted_ref, rows_ref, out_ref):
    for g in range(GROUPS):
        block = jnp.dot(
            to_sorted_ref[...],
            rows_ref[g * GROUP : (g + 1) * GROUP, :],
            preferred_element_type=F32,
        ).astype(BF)
        for k in range(4):
            for n in range(8):
                at = lanes(n)
                out_ref[k, g * KIND : (g + 1) * KIND, n * 256 : (n + 1) * 256] = block[
                    k * KIND : (k + 1) * KIND, at : at + 256
                ]


def sort_rows(to_sorted, rows):
    return pl.pallas_call(
        sort_kernel,
        out_shape=pltpu.VMEM((4, SLOTS, D), BF),
        in_specs=whole(2),
        out_specs=pl.BlockSpec(memory_space=VMEM),
        compiler_params=params(),
        name="sort_rows",
    )(to_sorted, rows)


def expert_kernel(rows_ref, to_natural_ref, *refs):
    pieces, (out_ref, in_mats, down_mat, sem) = refs[: Z + 1], refs[Z + 1 :]
    me = (lax.axis_index("H") * B + lax.axis_index("B")) * A + lax.axis_index("A")
    copies = []
    for k in range(Z):
        z = (me - k) & (Z - 1)
        h, b, q = z >> 3, (z >> 2) & 1, z & 3
        if k == Z // 2:
            parts = [((c,), (), pieces[k if c == 0 else Z]) for c in range(2)]
        else:
            every = slice(None)
            parts = [((every,), (every,), pieces[k])]
        for to, lead, ref in parts:
            for m in range(2):
                for f in range(3):
                    copies.append(
                        pltpu.make_async_copy(
                            ref.at[(*lead, slice(None), m, pl.ds(f * 32, 32))],
                            in_mats.at[
                                (b, m, *to, slice(None), h, q, slice(None), pl.ds(f * 128, 128))
                            ],
                            sem,
                        )
                    )
            copies.append(
                pltpu.make_async_copy(
                    ref.at[(*lead, slice(None), 2)], down_mat.at[(b, *to, slice(None), h, q)], sem
                )
            )
    for copy in copies:
        copy.start()
    for copy in copies:
        copy.wait()

    def down_chunk(b, k):
        c, x = k // X, k % X
        return jnp.concatenate(
            [down_mat[b, c, x, h].reshape(FW, 128) for h in range(H)], axis=1
        )

    inner, d_gate, d_up = [], [], []
    for b in range(B):
        rows = rows_ref[b]
        gate_pre = jnp.dot(rows, in_mats[b, 0].reshape(D, FW), preferred_element_type=F32)
        up_pre = jnp.dot(rows, in_mats[b, 1].reshape(D, FW), preferred_element_type=F32)
        back = jnp.zeros((SLOTS, FW), F32)
        for k in range(8):
            chunk = down_chunk(b, k)
            back = back + lax.dot_general(
                rows_ref[2 + b, :, k * 256 : (k + 1) * 256],
                chunk,
                (((1,), (1,)), ((), ())),
                preferred_element_type=F32,
            )
        s = jax.nn.sigmoid(gate_pre)
        silu = gate_pre * s
        inner.append((silu * up_pre).astype(BF))
        d_gate.append((back * up_pre * s * (1.0 + gate_pre * (1.0 - s))).astype(BF))
        d_up.append((back * silu).astype(BF))
    for k in range(8):
        parts = []
        for b in range(B):
            chunk = down_chunk(b, k)
            parts.append(jnp.dot(inner[b], chunk, preferred_element_type=F32).astype(BF))
        for b in range(B):
            total = lax.dot_general(
                d_gate[b],
                in_mats[b, 0, k // X, k % X].reshape(256, FW),
                (((1,), (1,)), ((), ())),
                preferred_element_type=F32,
            ) + lax.dot_general(
                d_up[b],
                in_mats[b, 1, k // X, k % X].reshape(256, FW),
                (((1,), (1,)), ((), ())),
                preferred_element_type=F32,
            )
            parts.append(total.astype(BF))
        for g in range(GROUPS):
            block = jnp.concatenate([p[g * KIND : (g + 1) * KIND] for p in parts], axis=0)
            out_ref[g * GROUP : (g + 1) * GROUP, lanes(k) : lanes(k) + 256] = jnp.dot(
                to_natural_ref[...], block, preferred_element_type=F32
            ).astype(BF)


def experts(rows, to_natural, weights):
    return pl.pallas_call(
        expert_kernel,
        out_shape=pltpu.VMEM((ROWS, D), BF),
        in_specs=whole(2) + [pl.BlockSpec(memory_space=pl.ANY)] * (Z + 1),
        out_specs=pl.BlockSpec(memory_space=VMEM),
        scratch_shapes=[
            VMEM((B, 2, C, X, H, A, 32, FW), BF),
            VMEM((B, C, X, H, A, 96, 128), BF),
            pltpu.SemaphoreType.DMA,
        ],
        compiler_params=params(36),
        name="experts",
    )(rows, to_natural, *weights)


def combine_kernel(ids_ref, codes_ref, ret_ref, hidden_ref, gain_ref, grad_ref, out_ref, gin_ref):
    r0, r1 = route_rows(ids_ref[0:1, :], ids_ref[1:2, :])
    codes = codes_ref[...].astype(F32)
    weights = codes / (codes[0:1, :] + codes[1:2, :])
    lines = jnp.concatenate(
        [r0.astype(F32), r1.astype(F32), weights, jnp.zeros((TOK - 4, TOK), F32)], axis=0
    )
    columns = jnp.transpose(lines)
    c0, c1 = columns[:, 0:1].astype(I32), columns[:, 1:2].astype(I32)
    w0, w1 = columns[:, 2:3], columns[:, 3:4]
    at = lax.broadcasted_iota(I32, (TOK, ROWS), 1)
    one, zero = jnp.ones((TOK, ROWS), F32), jnp.zeros((TOK, ROWS), F32)
    chosen = jnp.concatenate(
        [
            jnp.where(at == c + shift, one, zero).astype(BF)
            for shift in (0, 2 * CAP)
            for c in (c0, c1)
        ],
        axis=0,
    )
    picked = jnp.dot(chosen, ret_ref[...], preferred_element_type=F32)
    mixture = picked[0:TOK] * w0 + picked[TOK : 2 * TOK] * w1
    grad_normed = picked[2 * TOK : 3 * TOK] * w0 + picked[3 * TOK :] * w1
    hidden = hidden_ref[...].astype(F32)
    row_scale = row_scale_of(hidden)
    out_ref[...] = (hidden + mixture).astype(BF)
    scaled = gain_ref[...] * grad_normed
    inner_mean = jnp.mean(scaled * hidden, axis=1, keepdims=True)
    gin_ref[...] = (
        grad_ref[...].astype(F32)
        + row_scale * scaled
        - hidden * ((row_scale * row_scale * row_scale) * inner_mean)
    ).astype(BF)


def combine(ids, codes, returned, hidden, gain, grad):
    shape = jax.ShapeDtypeStruct((TOK, D), BF)
    return pl.pallas_call(
        combine_kernel,
        out_shape=(shape, shape),
        in_specs=whole(6),
        out_specs=tuple(whole(2)),
        compiler_params=params(),
        name="combine",
    )(ids, codes, returned, hidden, gain, grad)


def exchange(rows):
    blocks = rows.reshape(PEERS, PER, D)
    return lax.all_to_all(blocks, ("X", "C", "Y"), 0, 0, tiled=True).reshape(ROWS, D)


def body(hidden_in, norm_gain, w_gate, w_up, w_down, expert_ids, gate_codes, out_grad):
    gain = norm_gain.reshape(1, D)
    ids, codes = expert_ids.T, gate_codes.T
    to_natural = sort_matrix()
    pieces = place(send_home(split_weights(w_gate, w_up, w_down)))
    weights = around(lax.all_to_all(pieces, "C", 0, 0, tiled=True))
    sent = dispatch(ids, hidden_in, gain, out_grad)
    arrived = exchange(sent)
    rows = sort_rows(jnp.asarray(to_natural.T, BF), arrived)
    rows = pltpu.with_memory_space_constraint(rows, VMEM)
    results = experts(rows, jnp.asarray(to_natural, BF), weights)
    returned = exchange(results)
    return combine(ids, codes, returned, hidden_in, gain, out_grad)


def solution(mesh):
    fine = Mesh(mesh.devices.reshape(X, C, H, B, A, Y), ("X", "C", "H", "B", "A", "Y"))
    tokens = P(("X", "C", "H", "B", "A", "Y"), None)
    owner, feature = ("B", "A", "Y"), ("X", "C", "H")
    in_specs = (
        tokens,
        P(),
        P(owner, feature, None),
        P(owner, feature, None),
        P(owner, None, feature),
        tokens,
        tokens,
        tokens,
    )
    return jax.shard_map(
        body, mesh=fine, in_specs=in_specs, out_specs=(tokens, tokens), check_vma=False
    )
```
